32 devices in a mesh: grp: 4 (over z), dev: 8 (over y, x, core).
Axes of the slice: x: 2, y: 2, z: 4, core: 2. Of those that a mesh axis runs over, the one named last changes fastest.
Arguments:
- vertex_values: bfloat16 [2048, 128, 256], P(('grp', 'dev')), may hold values from -6 to 6
- position_domain_label: int32 [2048], P(('grp', 'dev')), may hold values from 0 to 64, as said below
- position_vertex_tally: int32 [2048], P(('grp', 'dev')), may hold values from 0 to 128, as said below
- normalizer_gain: float32 [256], replicated, may hold values from 0.1 to 1.9
- embedding_matrix: bfloat16 [256, 256], replicated, may hold values from -0.375 to 0.375
- partition_input_matrix: bfloat16 [256, 256], replicated, may hold values from -0.375 to 0.375
- partition_score_matrix: bfloat16 [32, 64], replicated, may hold values from -60 to 60
- softmax_sharpness: float32 [8], replicated, may hold values from 0.3 to 1
- partition_attention_maps: float32 [3, 32, 32], replicated, may hold values from -10 to 10
- readout_matrix: bfloat16 [256, 256], replicated, may hold values from -1.5 to 1.5
Outputs:
- updated: bfloat16 [2048, 128, 256], P(('grp', 'dev'))
The draws below stay inside these ranges and needn't reach their ends.
Inputs may be any that keep to these rules, and one draw needn't show every extreme that they name: `position_domain_label`: on each device the used slots come first; a device may use none. Reading the devices in order and their used slots in order lists every mesh's blocks as one run, meshes in increasing order, each mesh 2 or more blocks. Exactly 1024 slots are used in all, and some device uses all 64 of its slots. `position_vertex_tally`: 128 in every used slot except the last block of each mesh, which holds 1 to 128; 0 in unused slots.
All inputs are finite; a program needn't handle non-finite values.
Results may differ from the reference program's by a relative error of at most 0.012.
The reference program's roundings to bfloat16 on the way count: a program that leaves them out, or rounds other values in their place, can miss the bound.
Values may be sent and summed in bfloat16 or wider, within the bound.
A program may use at most 128 MiB of HBM per device.

```python
import math
import jax
import jax.numpy as jnp
from jax import lax

C = 256
ATTENTION_GROUPS = 8
DH = 32
M = 64
BLOCK = 128
SLOTS = 64
OWN = 32
MESHES = 64
N_GRP = 4
N_DEV = 8
DEVICES = 32


def layout_tables(key):
    device_count = N_GRP * N_DEV
    half_count = device_count // 2
    block_total = device_count * OWN
    key_bridge, key_full, key_moves, key_heavy, key_last = jax.random.split(jax.random.fold_in(key, 7), 5)
    bridge = jax.random.randint(key_bridge, (), 0, half_count - 1).astype(jnp.int32)
    device = jnp.arange(device_count, dtype=jnp.int32)
    vacant = (device > bridge) & (device < bridge + half_count)
    active = jnp.logical_not(vacant)
    active_rank = jnp.cumsum(active.astype(jnp.int32)) - 1
    full_rank = jax.random.randint(key_full, (), 0, half_count + 1).astype(jnp.int32)
    is_full = active & (active_rank == full_rank)
    others = active & jnp.logical_not(is_full)
    other_rank = (jnp.cumsum(others.astype(jnp.int32)) - 1).astype(jnp.int32)
    share = (block_total - SLOTS) // half_count
    leftover = block_total - SLOTS - share * half_count
    base = share + (other_rank < leftover).astype(jnp.int32)
    limit = max(0, min(share // 2, SLOTS - share - 1))
    pair_moves = jax.random.randint(key_moves, (device_count,), 0, limit + 1).astype(jnp.int32)
    pair_id = jnp.clip(other_rank // 2, 0, device_count - 1)
    delta = pair_moves[pair_id]
    even = other_rank % 2 == 0
    partnered = jnp.logical_or(jnp.logical_not(even), other_rank + 1 < half_count)
    signed = jnp.where(even, delta, -delta) * partnered.astype(jnp.int32)
    used_slots = jnp.where(is_full, SLOTS, jnp.where(others, base + signed, 0)).astype(jnp.int32)
    run_ends = jnp.cumsum(used_slots).astype(jnp.int32)
    starts = run_ends - used_slots
    bridge_start = run_ends[bridge] - 1
    heavy = jax.random.randint(key_heavy, (MESHES,), 1, 9).astype(jnp.int32)
    heavy = heavy * heavy * heavy
    middle = jnp.clip(bridge_start * (MESHES - 1) // block_total, 1, MESHES - 2).astype(jnp.int32)
    index = jnp.arange(MESHES, dtype=jnp.int32)
    before = index < middle
    after = index > middle
    rest_after = block_total - bridge_start - 2
    heavy_before = jnp.sum(jnp.where(before, heavy, 0))
    heavy_after = jnp.sum(jnp.where(after, heavy, 0))
    size_before = 2 + (bridge_start - 2 * middle) * heavy // heavy_before
    size_after = 2 + (rest_after - 2 * (MESHES - 1 - middle)) * heavy // heavy_after
    mesh_blocks = jnp.where(before, size_before, jnp.where(after, size_after, 2)).astype(jnp.int32)
    short_before = bridge_start - jnp.sum(jnp.where(before, mesh_blocks, 0))
    short_after = rest_after - jnp.sum(jnp.where(after, mesh_blocks, 0))
    mesh_blocks = mesh_blocks + jnp.where(index == middle - 1, short_before, 0) + jnp.where(index == MESHES - 1, short_after, 0)
    mesh_ends = jnp.cumsum(mesh_blocks).astype(jnp.int32)
    column = jnp.arange(SLOTS, dtype=jnp.int32)[None, :]
    global_block = starts[:, None] + column
    in_use = column < used_slots[:, None]
    mesh_of = jnp.sum((mesh_ends[None, None, :] <= global_block[:, :, None]).astype(jnp.int32), axis=2)
    clipped = jnp.minimum(mesh_of, MESHES - 1)
    last_size = jax.random.randint(key_last, (MESHES,), 1, BLOCK + 1).astype(jnp.int32)
    is_last = global_block == mesh_ends[clipped] - 1
    filled = jnp.where(is_last, last_size[clipped], BLOCK)
    position_domain_label = jnp.where(in_use, mesh_of, MESHES).reshape(-1).astype(jnp.int32)
    position_vertex_tally = jnp.where(in_use, filled, 0).reshape(-1).astype(jnp.int32)
    return (position_domain_label, position_vertex_tally)


def draw_position_domain_label(key, part):
    return layout_tables(key)[0]


def draw_position_vertex_tally(key, part):
    return layout_tables(key)[1]


def draw_partition_score_matrix(key, part):
    base = jnp.clip(jax.random.normal(jax.random.fold_in(key, 11), (DH, M), jnp.float32), -3.0, 3.0) / math.sqrt(DH)
    return base.astype(jnp.bfloat16)


def draw_partition_attention_maps(key, part):
    base = jnp.clip(jax.random.normal(jax.random.fold_in(key, 17), (3, DH, DH), jnp.float32), -3.0, 3.0) / math.sqrt(DH)
    return base


def block_levels(own_key, extent, pieces, smallest, top_value):
    def one(axis_at, blocks):
        heights = jax.random.uniform(jax.random.fold_in(jax.random.fold_in(own_key, 6), axis_at), (blocks,), jnp.float32, smallest / len(pieces), top_value / len(pieces))
        return jnp.repeat(jnp.exp(heights), extent[axis_at] // blocks).reshape((-1,) + (1,) * (len(extent) - axis_at - 1))

    gain = one(*pieces[0])
    for cut in pieces[1:]:
        gain = gain * one(*cut)
    return gain


def scatter_about(stream_key, shape, scale, bound, cuts=(), held_as=jnp.bfloat16):
    gain = block_levels(stream_key, shape, cuts, -0.22, 0.18) if cuts else 1.0
    values = jax.random.normal(stream_key, shape, jnp.float32) * scale * gain
    return jnp.minimum(jnp.maximum(values, -bound), bound).astype(held_as)


def setup_inputs(seed: int = 0) -> dict:
    key_list = jax.random.split(jax.random.key(seed), 11)
    return {
        "vertex_values": scatter_about(key_list[0], (DEVICES * SLOTS, BLOCK, C), 1.0, 6.0, ((0, 32),)),
        "position_domain_label": draw_position_domain_label(jax.random.fold_in(key_list[10], 71), 0),
        "position_vertex_tally": draw_position_vertex_tally(jax.random.fold_in(key_list[10], 71), 0),
        "normalizer_gain": jnp.clip(1.0 + 0.18 * jax.random.normal(key_list[3], (C,), jnp.float32), 0.1, 1.9),
        "embedding_matrix": scatter_about(key_list[4], (C, C), C ** -0.5, 0.375),
        "partition_input_matrix": scatter_about(key_list[5], (C, C), C ** -0.5, 0.375),
        "partition_score_matrix": draw_partition_score_matrix(jax.random.fold_in(key_list[10], 71), 0),
        "softmax_sharpness": jnp.clip(jnp.exp(jax.random.uniform(key_list[7], (ATTENTION_GROUPS,), jnp.float32, math.log(0.3), math.log(1.0))), 0.3, 1.0),
        "partition_attention_maps": draw_partition_attention_maps(jax.random.fold_in(key_list[10], 71), 0),
        "readout_matrix": scatter_about(key_list[9], (C, C), (C // 16) ** -0.5, 1.5),
    }


HIGHEST_PRECISION = lax.Precision.HIGHEST

def partition_routine(tile_sequence, vertex_tallies, domain_sequence, normalizer_gain, embedding_matrix, partition_input_matrix, partition_score_matrix, softmax_sharpness):
    tile_amount, tile_height, model_width = tile_sequence.shape
    attention_group_amount = softmax_sharpness.shape[0]
    head_width = model_width // attention_group_amount
    partition_amount = partition_score_matrix.shape[1]
    flattened = tile_sequence.reshape(tile_amount * tile_height, model_width).astype(jnp.float32)
    centre = flattened - lax.optimization_barrier(jnp.mean(flattened, axis=1, keepdims=True))
    spread = lax.optimization_barrier(jnp.mean(centre * centre, axis=1, keepdims=True))
    normed = (centre * lax.rsqrt(spread + 1e-05) * normalizer_gain).astype(jnp.bfloat16)
    features = jnp.dot(normed, embedding_matrix, preferred_element_type=jnp.float32).astype(jnp.bfloat16)
    middles = jnp.dot(normed, partition_input_matrix, preferred_element_type=jnp.float32).astype(jnp.bfloat16)
    partition_scores = jnp.dot(middles.reshape(-1, head_width), partition_score_matrix, preferred_element_type=jnp.float32)
    partition_scores = partition_scores.reshape(tile_amount, tile_height, attention_group_amount, partition_amount) / softmax_sharpness[:, None]
    living = (lax.broadcasted_iota(jnp.int32, (tile_amount, tile_height), 1) < vertex_tallies[:, None]).astype(jnp.float32)
    partition_shares = (jax.nn.softmax(partition_scores, axis=-1) * living[:, :, None, None]).astype(jnp.bfloat16)
    partial_sums = jnp.einsum('bphm,bphd->bhmd', partition_shares.astype(jnp.float32), features.reshape(tile_amount, tile_height, attention_group_amount, head_width).astype(jnp.float32), precision=HIGHEST_PRECISION)
    partial_totals = lax.optimization_barrier(jnp.sum(partition_shares.astype(jnp.float32), axis=1))
    one_hot = (domain_sequence[:, None] == lax.broadcasted_iota(jnp.int32, (tile_amount, MESHES), 1)).astype(jnp.float32)
    domain_accumulated = jnp.dot(one_hot.T, partial_sums.reshape(tile_amount, -1), precision=HIGHEST_PRECISION)
    domain_share_accumulated = jnp.dot(one_hot.T, partial_totals.reshape(tile_amount, -1), precision=HIGHEST_PRECISION)
    return (partition_shares.reshape(tile_amount, tile_height, attention_group_amount * partition_amount), domain_accumulated, domain_share_accumulated)

def attend_tokens(domain_accumulated, domain_share_accumulated, partition_attention_maps):
    row_count, partition_amount = domain_share_accumulated.shape
    head_width = partition_attention_maps.shape[1]
    tokens = domain_accumulated.reshape(row_count, partition_amount, head_width) / (domain_share_accumulated[:, :, None] + 1.0)
    queries = jnp.einsum('rmd,de->rme', tokens, partition_attention_maps[0], precision=HIGHEST_PRECISION)
    key_rows = jnp.einsum('rmd,de->rme', tokens, partition_attention_maps[1], precision=HIGHEST_PRECISION)
    values = jnp.einsum('rmd,de->rme', tokens, partition_attention_maps[2], precision=HIGHEST_PRECISION)
    scores = jnp.einsum('rme,rne->rmn', queries, key_rows, precision=HIGHEST_PRECISION) * head_width ** (-0.5)
    token_probs = jax.nn.softmax(scores, axis=-1)
    blended = jnp.einsum('rmn,rne->rme', token_probs, values, precision=HIGHEST_PRECISION)
    return blended.reshape(row_count, partition_amount * head_width).astype(jnp.bfloat16)

def spread_phase(tile_sequence, vertex_tallies, domain_sequence, partition_shares, tokens, readout_matrix):
    tile_amount, tile_height, model_width = tile_sequence.shape
    attention_group_amount = tokens.shape[0] // MESHES
    partition_amount = partition_shares.shape[2] // attention_group_amount
    head_width = model_width // attention_group_amount
    tables = tokens.reshape(MESHES, attention_group_amount, partition_amount, head_width)
    chosen = jnp.take(tables, jnp.minimum(domain_sequence, MESHES - 1), axis=0)
    blended = jnp.einsum('bphm,bhmd->bphd', partition_shares.reshape(tile_amount, tile_height, attention_group_amount, partition_amount).astype(jnp.float32), chosen.astype(jnp.float32), precision=HIGHEST_PRECISION).astype(jnp.bfloat16)
    projected = jnp.dot(blended.reshape(-1, model_width), readout_matrix, preferred_element_type=jnp.float32)
    living = (lax.broadcasted_iota(jnp.int32, (tile_amount, tile_height), 1) < vertex_tallies[:, None]).astype(jnp.float32)
    result = (tile_sequence.reshape(-1, model_width).astype(jnp.float32) + projected) * living.reshape(-1, 1)
    return result.reshape(tile_amount, tile_height, model_width).astype(jnp.bfloat16)

def reference(vertex_values, position_domain_label, position_vertex_tally, normalizer_gain, embedding_matrix, partition_input_matrix, partition_score_matrix, softmax_sharpness, partition_attention_maps, readout_matrix):
    used_slots = lax.optimization_barrier(jnp.sum((position_domain_label < MESHES).astype(jnp.int32).reshape(DEVICES, SLOTS), axis=1))
    run_ends = jnp.cumsum(used_slots).astype(jnp.int32)
    starts = run_ends - used_slots
    block_total = DEVICES * OWN
    global_index = jnp.arange(block_total, dtype=jnp.int32)
    source = lax.optimization_barrier(jnp.sum((run_ends[None, :] <= global_index[:, None]).astype(jnp.int32), axis=1))
    home_rows = (source * SLOTS + global_index - starts[source]).astype(jnp.int32)
    group_count = block_total // 64
    tile_sequence = vertex_values[home_rows].reshape(group_count, 64, BLOCK, C)
    vertex_tallies = position_vertex_tally[home_rows].reshape(group_count, 64)
    domain_sequence = position_domain_label[home_rows].reshape(group_count, 64)

    def gather_step(running, lookup_element):
        vacant_position_flags, domain_accumulated, domain_share_accumulated = partition_routine(lookup_element[0], lookup_element[1], lookup_element[2], normalizer_gain, embedding_matrix, partition_input_matrix, partition_score_matrix, softmax_sharpness)
        return ((running[0] + domain_accumulated, running[1] + domain_share_accumulated), None)
    initial = (jnp.zeros((MESHES, C * M), jnp.float32), jnp.zeros((MESHES, ATTENTION_GROUPS * M), jnp.float32))
    (domain_accumulated, domain_share_accumulated), vacant_position_flags = lax.scan(gather_step, initial, (tile_sequence, vertex_tallies, domain_sequence))
    tokens = attend_tokens(domain_accumulated.reshape(MESHES * ATTENTION_GROUPS, -1), domain_share_accumulated.reshape(MESHES * ATTENTION_GROUPS, -1), partition_attention_maps)

    def spread_step(lookup_element):
        partition_shares = partition_routine(lookup_element[0], lookup_element[1], lookup_element[2], normalizer_gain, embedding_matrix, partition_input_matrix, partition_score_matrix, softmax_sharpness)[0]
        return spread_phase(lookup_element[0], lookup_element[1], lookup_element[2], partition_shares, tokens, readout_matrix)
    results = lax.map(spread_step, (tile_sequence, vertex_tallies, domain_sequence))
    return jnp.zeros_like(vertex_values).at[home_rows].set(results.reshape(block_total, BLOCK, C))
```

```python
import functools
import math

import jax
import jax.numpy as jnp
from jax import lax
from jax.experimental import pallas as pl
from jax.experimental.pallas import tpu as pltpu
from jax.sharding import PartitionSpec as P

MESHES = 64
CHUNK = 4
MESH_ID = pl.DeviceIdType.MESH
NT = (((1,), (1,)), ((), ()))
F32 = jnp.float32
BF16 = jnp.bfloat16


def dot(a, b):
    return jnp.dot(a, b, preferred_element_type=F32)


def dot_nt(a, b):
    return lax.dot_general(a, b, NT, preferred_element_type=F32)


def halves(x):
    high = x.astype(BF16)
    return high, (x - high.astype(F32)).astype(BF16)


def dot3(a, b, product=dot):
    return product(a[0], b[0]) + (product(a[0], b[1]) + product(a[1], b[0]))


def lanes(shape):
    return lax.broadcasted_iota(jnp.int32, shape, len(shape) - 1)


def gather_kernel(
    heads,
    label_ref,
    tally_ref,
    x_ref,
    gain_ref,
    embed_ref,
    inputs_t_ref,
    score_t_ref,
    sharp_ref,
    shares_ref,
    sums_ref,
    ends_ref,
    running_ref,
):
    step = pl.program_id(0)
    chunk, height, width = x_ref.shape
    points = chunk * height
    parts = score_t_ref.shape[0] // heads
    half = width // 2
    group = heads // 2

    @pl.when(step == 0)
    def _():
        running_ref[...] = jnp.zeros_like(running_ref)
        ends_ref[...] = jnp.zeros_like(ends_ref)
        used = label_ref[0] < MESHES
        ends_ref[0, parts:] = jnp.full(
            ends_ref.shape[1:], label_ref[0].astype(F32), F32
        )[parts:]
        ends_ref[1, parts:] = jnp.full_like(ends_ref[1, parts:], -1.0)

    x = x_ref[...].reshape(points, width).astype(F32)
    centre = x - jnp.mean(x, axis=1, keepdims=True)
    var = jnp.mean(centre * centre, axis=1, keepdims=True)
    normed = (centre * lax.rsqrt(var + 1e-05) * gain_ref[...]).astype(BF16)
    features = dot(normed, embed_ref[...]).astype(BF16)
    middles = dot_nt(inputs_t_ref[...], normed).astype(BF16)
    scores = dot(score_t_ref[...], middles)
    lane = lanes((1, height))
    living = jnp.concatenate(
        [
            (lane < tally_ref[step * chunk + b]).astype(F32)
            for b in range(chunk)
        ],
        axis=1,
    )
    for h in range(heads):
        rows = scores[h * parts : (h + 1) * parts]
        top = jnp.max(rows, axis=0, keepdims=True)
        powers = jnp.exp2((rows - top) * sharp_ref[h])
        scale = living / jnp.sum(powers, axis=0, keepdims=True)
        shares_ref[0, h * parts : (h + 1) * parts, :] = (powers * scale).astype(BF16)

    ones = jnp.ones((height, 128), BF16)
    share_lane = lanes((parts, half)) // (half // group)
    total_lane = lanes((parts, 128)) // (128 // heads)
    for b in range(chunk):
        slot = step * chunk + b
        label = label_ref[slot]
        before = label_ref[jnp.maximum(slot - 1, 0)]
        pieces = []
        totals = None
        for g in range(2):
            right = jnp.concatenate(
                [
                    features[b * height : (b + 1) * height, g * half : (g + 1) * half],
                    ones,
                ],
                axis=1,
            )
            got = dot(
                shares_ref[
                    0,
                    g * group * parts : (g + 1) * group * parts,
                    b * height : (b + 1) * height,
                ],
                right,
            )
            piece = got[:parts, :half]
            for i in range(group):
                mine = got[i * parts : (i + 1) * parts]
                piece = jnp.where(share_lane == i, mine[:, :half], piece)
                if totals is None:
                    totals = mine[:, half:]
                else:
                    totals = jnp.where(
                        total_lane == g * group + i, mine[:, half:], totals
                    )
            pieces.append(piece)
        new = jnp.concatenate(pieces + [totals], axis=1)
        keep = jnp.where(label == before, 1.0, 0.0)
        new = running_ref[...] * keep + new
        running_ref[...] = new
        sums_ref[b] = new

        @pl.when(label < MESHES)
        def _():
            ends_ref[1, :parts] = new
            ends_ref[1, parts:] = jnp.full_like(
                ends_ref[1, parts:], label.astype(F32)
            )

            @pl.when(label == label_ref[0])
            def _():
                ends_ref[0, :parts] = new


def exchange_kernel(axes, ends_ref, out_ref, held, sent, send_sem, recv_sem):
    parts = out_ref.shape[1]
    partners = []
    for name, size in reversed(axes):
        bit = 1
        while bit < size:
            at = {n: lax.axis_index(n) for n, _ in axes}
            here = at[name]
            at[name] = here + bit - 2 * bit * (here // bit % 2)
            partners.append(tuple(at[n] for n, _ in axes))
            bit *= 2
    barrier = pltpu.get_barrier_semaphore()
    for partner in partners:
        pl.semaphore_signal(barrier, inc=1, device_id=partner, device_id_type=MESH_ID)
    pl.semaphore_wait(barrier, len(partners))

    def load(ref, i):
        block = ref[i]
        return block[:parts].reshape(parts // 8, 8, -1), block[parts:]

    first, first_id = load(ends_ref, 0)
    last, last_id = load(ends_ref, 1)
    group_first, group_first_id, group_last, group_last_id = first, first_id, last, last_id
    for i, partner in enumerate(partners):
        source = ends_ref if i == 0 else sent.at[i - 1]
        copy = pltpu.make_async_remote_copy(
            src_ref=source,
            dst_ref=held.at[i],
            send_sem=send_sem.at[i],
            recv_sem=recv_sem.at[i],
            device_id=partner,
            device_id_type=MESH_ID,
        )
        copy.start()
        copy.wait()
        other_first, other_first_id = load(held.at[i], 0)
        other_last, other_last_id = load(held.at[i], 1)

        def found(own_id):
            return jnp.where(
                (own_id == other_first_id)[None],
                other_first,
                jnp.where((own_id == other_last_id)[None], other_last, 0.0),
            )

        first = first + found(first_id)
        last = last + found(last_id)
        if i < len(partners) - 1:
            new_first_id = jnp.minimum(group_first_id, other_first_id)
            new_last_id = jnp.maximum(group_last_id, other_last_id)
            group_first = jnp.where(
                (group_first_id == new_first_id)[None], group_first, 0.0
            ) + jnp.where((other_first_id == new_first_id)[None], other_first, 0.0)
            group_last = jnp.where(
                (group_last_id == new_last_id)[None], group_last, 0.0
            ) + jnp.where((other_last_id == new_last_id)[None], other_last, 0.0)
            group_first_id, group_last_id = new_first_id, new_last_id
            sent[i, 0, :parts] = group_first.reshape(parts, -1)
            sent[i, 0, parts:] = group_first_id
            sent[i, 1, :parts] = group_last.reshape(parts, -1)
            sent[i, 1, parts:] = group_last_id
    out_ref[0] = first.reshape(parts, -1)
    out_ref[1] = last.reshape(parts, -1)


def spread_kernel(
    heads,
    label_ref,
    tally_ref,
    end_ref,
    x_ref,
    shares_ref,
    *refs,
):
    chunk, height, width = x_ref.shape
    sums_refs = refs[:chunk]
    ends_ref, expand_ref, map_high_ref, map_low_ref, readout_ref, out_ref, mixed_ref = refs[chunk:]
    step = pl.program_id(0)
    parts = ends_ref.shape[1]
    dim = width // heads
    last_label = end_ref[end_ref.shape[0] - 1]

    for b in range(chunk):
        slot = step * chunk + b
        label = label_ref[slot]
        fresh = jnp.logical_or(slot == 0, label != label_ref[jnp.maximum(slot - 1, 0)])

        @pl.when(jnp.logical_and(fresh, label < MESHES))
        def _():
            is_first = label == label_ref[0]
            is_last = label == last_label
            state = jnp.where(
                is_first,
                ends_ref[0],
                jnp.where(is_last, ends_ref[1], sums_refs[b][0]),
            )
            high, low = halves(state[:, width:])
            totals = dot(high, expand_ref[...]) + dot(low, expand_ref[...])
            tokens = state[:, :width] / (totals + 1.0)
            tokens = jnp.concatenate([tokens, tokens], axis=0)
            split = halves(tokens)
            maps = [(map_high_ref[i], map_low_ref[i]) for i in range(3)]
            queries = halves(dot3(split, maps[0]))
            keys = halves(dot3((split[0][:parts], split[1][:parts]), maps[1]))
            values = halves(dot3(maps[2], split, dot_nt))
            lane = lanes((parts, width)) // dim

            def stacked(k):
                return jnp.concatenate(
                    [jnp.where(lane == h, k, jnp.zeros_like(k)) for h in range(heads)],
                    axis=0,
                )

            scores = dot3(tuple(stacked(k) for k in keys), queries, dot_nt)
            probs = []
            factor = dim**-0.5 * math.log2(math.e)
            for h in range(heads):
                rows = scores[h * parts : (h + 1) * parts]
                top = jnp.max(rows, axis=0, keepdims=True)
                powers = jnp.exp2((rows - top) * factor)
                probs.append(powers / jnp.sum(powers, axis=0, keepdims=True))
            probs = halves(jnp.concatenate(probs, axis=0))
            row_head = lax.broadcasted_iota(jnp.int32, (width, 2 * parts), 0) // dim
            col_head = lanes((width, 2 * parts)) // parts

            def spaced(v):
                return jnp.concatenate(
                    [
                        jnp.where(row_head == col_head + 2 * t, v, jnp.zeros_like(v))
                        for t in range(heads // 2)
                    ],
                    axis=1,
                )

            mixed = dot3(tuple(spaced(v) for v in values), probs)
            mixed_ref[...] = spaced(mixed.astype(BF16))

        @pl.when(label < MESHES)
        def _():
            spread = dot(
                mixed_ref[...], shares_ref[0, :, b * height : (b + 1) * height]
            ).astype(BF16)
            projected = dot(spread.T, readout_ref[...])
            row = lax.broadcasted_iota(jnp.int32, (height, width), 0)
            result = jnp.where(
                row < tally_ref[slot], x_ref[b].astype(F32) + projected, 0.0
            )
            out_ref[b] = result.astype(BF16)

        @pl.when(label >= MESHES)
        def _():
            out_ref[b] = jnp.zeros_like(out_ref[b])


def whole(array):
    rank = array.ndim
    return pl.BlockSpec(array.shape, lambda *_: (0,) * rank)


def on_device(
    axes,
    vertex_values,
    label,
    tally,
    gain,
    embedding_matrix,
    partition_input_matrix,
    partition_score_matrix,
    sharpness,
    maps,
    readout_matrix,
):
    slots, height, width = vertex_values.shape
    heads = sharpness.shape[0]
    dim = width // heads
    parts = partition_score_matrix.shape[1]
    steps = slots // CHUNK
    wide = width + 128
    points = CHUNK * height
    eye = jnp.eye(heads, dtype=F32)

    gain = gain.reshape(1, width)
    inputs_t = partition_input_matrix.T
    score_t = jnp.kron(eye.astype(BF16), partition_score_matrix.T)
    sharp = math.log2(math.e) / sharpness
    x_spec = pl.BlockSpec((CHUNK, height, width), lambda i, *_: (i, 0, 0))
    shares_spec = pl.BlockSpec((1, heads * parts, points), lambda i, *_: (i, 0, 0))
    ends_shape = (2, parts + 8, wide)
    shares, sums, ends = pl.pallas_call(
        functools.partial(gather_kernel, heads),
        grid_spec=pltpu.PrefetchScalarGridSpec(
            num_scalar_prefetch=2,
            grid=(steps,),
            in_specs=[
                x_spec,
                whole(gain),
                whole(embedding_matrix),
                whole(inputs_t),
                whole(score_t),
                pl.BlockSpec(memory_space=pltpu.SMEM),
            ],
            out_specs=[
                shares_spec,
                pl.BlockSpec((CHUNK, parts, wide), lambda i, *_: (i, 0, 0)),
                pl.BlockSpec(ends_shape, lambda *_: (0, 0, 0)),
            ],
            scratch_shapes=[pltpu.VMEM((parts, wide), F32)],
        ),
        out_shape=[
            jax.ShapeDtypeStruct((steps, heads * parts, points), BF16),
            jax.ShapeDtypeStruct((slots, parts, wide), F32),
            jax.ShapeDtypeStruct(ends_shape, F32),
        ],
        name="gather",
    )(label, tally, vertex_values, gain, embedding_matrix, inputs_t, score_t, sharp)

    rounds = sum(size.bit_length() - 1 for _, size in axes)
    totals = pl.pallas_call(
        functools.partial(exchange_kernel, axes),
        out_shape=jax.ShapeDtypeStruct((2, parts, wide), F32),
        in_specs=[pl.BlockSpec(memory_space=pltpu.VMEM)],
        out_specs=pl.BlockSpec(memory_space=pltpu.VMEM),
        scratch_shapes=[
            pltpu.VMEM((rounds,) + ends_shape, F32),
            pltpu.VMEM((rounds,) + ends_shape, F32),
            pltpu.SemaphoreType.DMA((rounds,)),
            pltpu.SemaphoreType.DMA((rounds,)),
        ],
        compiler_params=pltpu.CompilerParams(collective_id=0, has_side_effects=True),
        name="exchange",
    )(ends)

    places = jnp.arange(slots, dtype=jnp.int32)
    run_end = jnp.max(
        jnp.where(label[:, None] == label[None, :], places[None, :], 0), axis=1
    )
    last_label = jnp.max(jnp.where(label < MESHES, label, -1), keepdims=True)
    end = jnp.concatenate([run_end, last_label]).astype(jnp.int32)
    blocks = jnp.stack(
        [jnp.kron(eye, maps[0]), jnp.kron(eye, maps[1]), jnp.kron(eye, maps[2].T)]
    )
    map_high, map_low = halves(blocks)
    expand = (
        jnp.arange(128)[:, None] == (128 // heads) * (jnp.arange(width)[None, :] // dim)
    ).astype(BF16)

    def sums_spec(b):
        return pl.BlockSpec(
            (1, parts, wide), lambda i, l, t, e: (e[i * CHUNK + b], 0, 0)
        )

    return pl.pallas_call(
        functools.partial(spread_kernel, heads),
        grid_spec=pltpu.PrefetchScalarGridSpec(
            num_scalar_prefetch=3,
            grid=(steps,),
            in_specs=[x_spec, shares_spec]
            + [sums_spec(b) for b in range(CHUNK)]
            + [
                whole(totals),
                whole(expand),
                whole(map_high),
                whole(map_low),
                whole(readout_matrix),
            ],
            out_specs=x_spec,
            scratch_shapes=[pltpu.VMEM((width, heads * parts), BF16)],
        ),
        out_shape=jax.ShapeDtypeStruct(vertex_values.shape, BF16),
        name="spread",
    )(
        label,
        tally,
        end,
        vertex_values,
        shares,
        *([sums] * CHUNK),
        totals,
        expand,
        map_high,
        map_low,
        readout_matrix,
    )


def solution(mesh):
    axes = tuple((name, mesh.shape[name]) for name in mesh.axis_names)
    split = P(mesh.axis_names)
    points = P(mesh.axis_names, None, None)
    return jax.shard_map(
        functools.partial(on_device, axes),
        mesh=mesh,
        in_specs=(points, split, split) + (P(),) * 7,
        out_specs=points,
        check_vma=False,
    )
```

```python
import functools
import math

import jax
import jax.numpy as jnp
from jax import lax
from jax.experimental import pallas as pl
from jax.experimental.pallas import tpu as pltpu
from jax.sharding import PartitionSpec as P

MESHES = 64
CHUNK = 4
MESH_ID = pl.DeviceIdType.MESH
NT = (((1,), (1,)), ((), ()))
F32 = jnp.float32
BF16 = jnp.bfloat16
LOG2E = math.log2(math.e)


def dot(a, b):
    return jnp.dot(a, b, preferred_element_type=F32)


def dot_nt(a, b):
    return lax.dot_general(a, b, NT, preferred_element_type=F32)


def halves(x):
    high = x.astype(BF16)
    return high, (x - high.astype(F32)).astype(BF16)


def dot3(a, b, product=dot):
    return product(a[0], b[0]) + (product(a[0], b[1]) + product(a[1], b[0]))


def lanes(shape):
    return lax.broadcasted_iota(jnp.int32, shape, len(shape) - 1)


def tiler(dim, width):
    row = lax.broadcasted_iota(jnp.int32, (dim, width), 0)
    return (row == lanes((dim, width)) % dim).astype(BF16)


def gather_kernel(
    heads,
    label_ref,
    tally_ref,
    x_ref,
    gain_ref,
    embed_ref,
    inputs_ref,
    score_ref,
    sharp_ref,
    shares_ref,
    sums_ref,
    ends_ref,
    end_ref,
    running_ref,
    inputs_t_ref,
    score_t_ref,
):
    step = pl.program_id(0)
    chunk, height, width = x_ref.shape
    points = chunk * height
    dim, parts = score_ref.shape
    half = width // 2
    group = heads // 2
    slots = label_ref.shape[0]

    @pl.when(step == 0)
    def _():
        running_ref[...] = jnp.zeros_like(running_ref)
        ends_ref[...] = jnp.zeros_like(ends_ref)
        inputs_t_ref[...] = inputs_ref[...].T
        tiled = lax.dot_general(
            score_ref[...],
            tiler(dim, width),
            (((0,), (0,)), ((), ())),
            preferred_element_type=F32,
        )
        lane = lanes((parts, width)) // dim
        for h in range(heads):
            score_t_ref[h * parts : (h + 1) * parts] = jnp.where(
                lane == h, tiled, 0.0
            ).astype(BF16)

        def note(i, carry):
            follower, last, order = carry
            k = slots - 1 - i
            here = label_ref[k]
            differs = here != label_ref[jnp.minimum(k + 1, slots - 1)]
            follower = jnp.where(differs, k, follower)
            order = order + differs.astype(jnp.int32)
            end_ref[k] = follower
            end_ref[slots + k] = order % chunk
            return follower, jnp.maximum(last, jnp.where(here < MESHES, here, -1)), order

        end_ref[2 * slots] = lax.fori_loop(
            0, slots, note, (jnp.int32(slots - 1), jnp.int32(-1), jnp.int32(0))
        )[1]

    x = x_ref[...].reshape(points, width).astype(F32)
    centre = x - jnp.mean(x, axis=1, keepdims=True)
    var = jnp.mean(centre * centre, axis=1, keepdims=True)
    normed = (centre * lax.rsqrt(var + 1e-05) * gain_ref[...]).astype(BF16)
    features = dot(normed, embed_ref[...]).astype(BF16)
    middles = dot_nt(inputs_t_ref[...], normed).astype(BF16)
    lane = lanes((1, height))
    living = jnp.concatenate(
        [
            (lane < tally_ref[step * chunk + b]).astype(F32)
            for b in range(chunk)
        ],
        axis=1,
    )
    for h in range(heads):
        rows = dot(
            score_t_ref[h * parts : (h + 1) * parts, h // group * half : (h // group + 1) * half],
            middles[h // group * half : (h // group + 1) * half],
        )
        top = jnp.max(rows, axis=0, keepdims=True)
        sharp = LOG2E / jnp.full((1, points), sharp_ref[h], F32)
        powers = jnp.exp2((rows - top) * sharp)
        scale = living / jnp.sum(powers, axis=0, keepdims=True)
        shares_ref[0, h * parts : (h + 1) * parts, :] = (powers * scale).astype(BF16)

    ones = jnp.ones((height, 128), BF16)
    share_lane = lanes((parts, half)) // dim
    total_lane = lanes((parts, 128))
    running = running_ref[...]
    for b in range(chunk):
        slot = step * chunk + b
        same = label_ref[slot] == label_ref[jnp.maximum(slot - 1, 0)]
        pieces = []
        totals = None
        for g in range(2):
            right = jnp.concatenate(
                [
                    features[b * height : (b + 1) * height, g * half : (g + 1) * half],
                    ones,
                ],
                axis=1,
            )
            got = dot(
                shares_ref[
                    0,
                    g * group * parts : (g + 1) * group * parts,
                    b * height : (b + 1) * height,
                ],
                right,
            )
            piece = got[:parts, :half]
            for i in range(group):
                mine = got[i * parts : (i + 1) * parts]
                piece = jnp.where(share_lane == i, mine[:, :half], piece)
                if totals is None:
                    totals = mine[:, half:]
                else:
                    totals = jnp.where(
                        total_lane == g * group + i, mine[:, half:], totals
                    )
            pieces.append(piece)
        running = jnp.where(same, running, 0.0) + jnp.concatenate(
            pieces + [totals], axis=1
        )
        sums_ref[b] = running
    running_ref[...] = running
    for b in range(chunk):
        slot = step * chunk + b
        label = label_ref[slot]
        stop = jnp.logical_and(label < MESHES, end_ref[slot] == slot)

        @pl.when(jnp.logical_and(stop, label == label_ref[0]))
        def _():
            ends_ref[0] = sums_ref[b]

        @pl.when(jnp.logical_and(stop, label == end_ref[2 * slots]))
        def _():
            ends_ref[1] = sums_ref[b]


def exchange_kernel(
    axes, heads, label_ref, end_ref, ends_ref, out_ref, held, sent, send_sem, recv_sem
):
    parts = out_ref.shape[1]
    width = out_ref.shape[2] - 128
    partners = []
    for name, size in reversed(axes):
        bit = 1
        while bit < size:
            at = {n: lax.axis_index(n) for n, _ in axes}
            here = at[name]
            at[name] = here + bit - 2 * bit * (here // bit % 2)
            partners.append(tuple(at[n] for n, _ in axes))
            bit *= 2
    barrier = pltpu.get_barrier_semaphore()
    for partner in partners:
        pl.semaphore_signal(barrier, inc=1, device_id=partner, device_id_type=MESH_ID)

    def own(i):
        totals = ends_ref[i, :, width:].T[:heads]
        totals = jnp.concatenate([totals, jnp.zeros((heads, width - parts), F32)], axis=1)
        full = jnp.concatenate([ends_ref[i, :, :width], totals], axis=0)
        return full.reshape(-1, 8, width)

    def put(i, k, values, ids):
        sent[i, k] = jnp.concatenate([values.reshape(-1, width), ids], axis=0).astype(BF16)

    def load(i, k):
        block = held[i, k].astype(F32)
        return block[: parts + heads].reshape(-1, 8, width), block[parts + heads :]

    first = group_first = own(0)
    last = group_last = own(1)
    ids = (8, width)
    first_id = group_first_id = jnp.full(ids, label_ref[0].astype(F32), F32)
    last_id = group_last_id = jnp.full(
        ids, end_ref[end_ref.shape[0] - 1].astype(F32), F32
    )
    put(0, 0, first, first_id)
    put(0, 1, last, last_id)
    pl.semaphore_wait(barrier, len(partners))
    for i, partner in enumerate(partners):
        copy = pltpu.make_async_remote_copy(
            src_ref=sent.at[i],
            dst_ref=held.at[i],
            send_sem=send_sem.at[i],
            recv_sem=recv_sem.at[i],
            device_id=partner,
            device_id_type=MESH_ID,
        )
        copy.start()
        copy.wait()
        other_first, other_first_id = load(i, 0)
        other_last, other_last_id = load(i, 1)
        if i < len(partners) - 1:
            new_first_id = jnp.minimum(group_first_id, other_first_id)
            new_last_id = jnp.maximum(group_last_id, other_last_id)
            group_first = jnp.where(
                (group_first_id == new_first_id)[None], group_first, 0.0
            ) + jnp.where((other_first_id == new_first_id)[None], other_first, 0.0)
            group_last = jnp.where(
                (group_last_id == new_last_id)[None], group_last, 0.0
            ) + jnp.where((other_last_id == new_last_id)[None], other_last, 0.0)
            group_first_id, group_last_id = new_first_id, new_last_id
            put(i + 1, 0, group_first, group_first_id)
            put(i + 1, 1, group_last, group_last_id)

    def found(i, own_id):
        other_first, other_first_id = load(i, 0)
        other_last, other_last_id = load(i, 1)
        return jnp.where(
            (own_id == other_first_id)[None],
            other_first,
            jnp.where((own_id == other_last_id)[None], other_last, 0.0),
        )

    for k, (total, own_id) in enumerate([(first, first_id), (last, last_id)]):
        for i in range(len(partners)):
            total = total + found(i, own_id)
        total = total.reshape(-1, width)
        rows = jnp.concatenate(
            [total[parts:, :128], jnp.zeros((128 - heads, 128), F32)], axis=0
        )
        out_ref[k] = jnp.concatenate([total[:parts], rows.T[:parts]], axis=1)


def spread_kernel(
    heads,
    label_ref,
    tally_ref,
    end_ref,
    x_ref,
    shares_ref,
    *refs,
):
    chunk, height, width = x_ref.shape
    sums_refs = refs[:chunk]
    ends_ref, maps_ref, readout_ref, out_ref, mixed_ref, map_ref = refs[chunk:]
    step = pl.program_id(0)
    parts = ends_ref.shape[1]
    dim = width // heads
    slots = label_ref.shape[0]
    last_label = end_ref[end_ref.shape[0] - 1]

    @pl.when(step == 0)
    def _():
        across = tiler(dim, width)
        row = lax.broadcasted_iota(jnp.int32, (width, dim), 0)
        down = (row % dim == lanes((width, dim))).astype(BF16)
        same = (
            lax.broadcasted_iota(jnp.int32, (width, width), 0) // dim
            == lanes((width, width)) // dim
        )
        for i in range(3):
            for j, part in enumerate(halves(maps_ref[i])):
                tall = dot(down, part) if i < 2 else dot_nt(down, part)
                map_ref[i, j] = jnp.where(same, dot(tall.astype(BF16), across), 0.0).astype(BF16)

    for b in range(chunk):
        slot = step * chunk + b
        label = label_ref[slot]
        fresh = jnp.logical_or(slot == 0, label != label_ref[jnp.maximum(slot - 1, 0)])

        @pl.when(jnp.logical_and(fresh, label < MESHES))
        def _():
            is_first = label == label_ref[0]
            is_last = label == last_label
            state = jnp.where(
                is_first,
                ends_ref[0],
                jnp.where(is_last, ends_ref[1], sums_refs[b][0]),
            )
            high, low = halves(state[:, width:])
            expand = (
                lax.broadcasted_iota(jnp.int32, (128, width), 0)
                == lanes((128, width)) // dim
            ).astype(BF16)
            totals = dot(high, expand) + dot(low, expand)
            tokens = state[:, :width] / (totals + 1.0)
            tokens = jnp.concatenate([tokens, tokens], axis=0)
            split = halves(tokens)
            maps = [(map_ref[i, 0], map_ref[i, 1]) for i in range(3)]
            queries = halves(dot3(split, maps[0]))
            keys = halves(dot3((split[0][:parts], split[1][:parts]), maps[1]))
            values = halves(dot3(maps[2], split, dot_nt))
            lane = lanes((parts, width)) // dim

            def stacked(k):
                return jnp.concatenate(
                    [jnp.where(lane == h, k, jnp.zeros_like(k)) for h in range(heads)],
                    axis=0,
                )

            scores = dot3(tuple(stacked(k) for k in keys), queries, dot_nt)
            probs = []
            factor = dim**-0.5 * LOG2E
            for h in range(heads):
                rows = scores[h * parts : (h + 1) * parts]
                top = jnp.max(rows, axis=0, keepdims=True)
                powers = jnp.exp2((rows - top) * factor)
                probs.append(powers / jnp.sum(powers, axis=0, keepdims=True))
            probs = halves(jnp.concatenate(probs, axis=0))
            row_head = lax.broadcasted_iota(jnp.int32, (width, 2 * parts), 0) // dim
            col_head = lanes((width, 2 * parts)) // parts

            def spaced(v):
                return jnp.concatenate(
                    [
                        jnp.where(row_head == col_head + 2 * t, v, jnp.zeros_like(v))
                        for t in range(heads // 2)
                    ],
                    axis=1,
                )

            mixed = dot3(tuple(spaced(v) for v in values), probs)
            mixed_ref[end_ref[slots + slot]] = spaced(mixed.astype(BF16))

    pieces = []
    for b in range(chunk):
        pieces.append(
            dot(
                mixed_ref[end_ref[slots + step * chunk + b]],
                shares_ref[0, :, b * height : (b + 1) * height],
            ).astype(BF16)
        )
    for b in range(chunk):
        projected = dot(pieces[b].T, readout_ref[...])
        row = lax.broadcasted_iota(jnp.int32, (height, width), 0)
        result = jnp.where(
            row < tally_ref[step * chunk + b], x_ref[b].astype(F32) + projected, 0.0
        )
        out_ref[b] = result.astype(BF16)


def whole(array):
    rank = array.ndim
    return pl.BlockSpec(array.shape, lambda *_: (0,) * rank)


def on_device(
    axes,
    vertex_values,
    label,
    tally,
    gain,
    embedding_matrix,
    partition_input_matrix,
    partition_score_matrix,
    sharpness,
    maps,
    readout_matrix,
):
    slots, height, width = vertex_values.shape
    heads = sharpness.shape[0]
    dim = width // heads
    parts = partition_score_matrix.shape[1]
    steps = slots // CHUNK
    wide = width + 128
    points = CHUNK * height
    gain = gain.reshape(1, width)
    x_spec = pl.BlockSpec((CHUNK, height, width), lambda i, *_: (i, 0, 0))
    shares_spec = pl.BlockSpec((1, heads * parts, points), lambda i, *_: (i, 0, 0))
    shares, sums, ends, end = pl.pallas_call(
        functools.partial(gather_kernel, heads),
        grid_spec=pltpu.PrefetchScalarGridSpec(
            num_scalar_prefetch=2,
            grid=(steps,),
            in_specs=[
                x_spec,
                whole(gain),
                whole(embedding_matrix),
                whole(partition_input_matrix),
                whole(partition_score_matrix),
                pl.BlockSpec(memory_space=pltpu.SMEM),
            ],
            out_specs=[
                shares_spec,
                pl.BlockSpec((CHUNK, parts, wide), lambda i, *_: (i, 0, 0)),
                pl.BlockSpec((2, parts, wide), lambda *_: (0, 0, 0)),
                pl.BlockSpec(memory_space=pltpu.SMEM),
            ],
            scratch_shapes=[
                pltpu.VMEM((parts, wide), F32),
                pltpu.VMEM((width, width), BF16),
                pltpu.VMEM((heads * parts, width), BF16),
            ],
        ),
        out_shape=[
            jax.ShapeDtypeStruct((steps, heads * parts, points), BF16),
            jax.ShapeDtypeStruct((slots, parts, wide), F32),
            jax.ShapeDtypeStruct((2, parts, wide), F32),
            jax.ShapeDtypeStruct((2 * slots + 1,), jnp.int32),
        ],
        name="gather",
    )(
        label,
        tally,
        vertex_values,
        gain,
        embedding_matrix,
        partition_input_matrix,
        partition_score_matrix,
        sharpness,
    )

    rounds = sum(size.bit_length() - 1 for _, size in axes)
    packet = (rounds, 2, parts + heads + 8, width)
    totals = pl.pallas_call(
        functools.partial(exchange_kernel, axes, heads),
        out_shape=jax.ShapeDtypeStruct((2, parts, wide), F32),
        in_specs=[
            pl.BlockSpec(memory_space=pltpu.SMEM),
            pl.BlockSpec(memory_space=pltpu.SMEM),
            pl.BlockSpec(memory_space=pltpu.VMEM),
        ],
        out_specs=pl.BlockSpec(memory_space=pltpu.VMEM),
        scratch_shapes=[
            pltpu.VMEM(packet, BF16),
            pltpu.VMEM(packet, BF16),
            pltpu.SemaphoreType.DMA((rounds,)),
            pltpu.SemaphoreType.DMA((rounds,)),
        ],
        compiler_params=pltpu.CompilerParams(collective_id=0, has_side_effects=True),
        name="exchange",
    )(label, end, ends)

    def sums_spec(b):
        return pl.BlockSpec(
            (1, parts, wide), lambda i, l, t, e: (e[i * CHUNK + b], 0, 0)
        )

    return pl.pallas_call(
        functools.partial(spread_kernel, heads),
        grid_spec=pltpu.PrefetchScalarGridSpec(
            num_scalar_prefetch=3,
            grid=(steps,),
            in_specs=[x_spec, shares_spec]
            + [sums_spec(b) for b in range(CHUNK)]
            + [
                whole(totals),
                whole(maps),
                whole(readout_matrix),
            ],
            out_specs=x_spec,
            scratch_shapes=[
                pltpu.VMEM((CHUNK, width, heads * parts), BF16),
                pltpu.VMEM((3, 2, width, width), BF16),
            ],
        ),
        out_shape=jax.ShapeDtypeStruct(vertex_values.shape, BF16),
        name="spread",
    )(
        label,
        tally,
        end,
        vertex_values,
        shares,
        *([sums] * CHUNK),
        totals,
        maps,
        readout_matrix,
    )


def solution(mesh):
    axes = tuple((name, mesh.shape[name]) for name in mesh.axis_names)
    split = P(mesh.axis_names)
    points = P(mesh.axis_names, None, None)
    return jax.shard_map(
        functools.partial(on_device, axes),
        mesh=mesh,
        in_specs=(points, split, split) + (P(),) * 7,
        out_specs=points,
        check_vma=False,
    )
```

```python
import functools
import math

import jax
import jax.numpy as jnp
from jax import lax
from jax.experimental import pallas as pl
from jax.experimental.pallas import tpu as pltpu
from jax.sharding import PartitionSpec as P

MESHES = 64
CHUNK = 4
MESH_ID = pl.DeviceIdType.MESH
NT = (((1,), (1,)), ((), ()))
F32 = jnp.float32
BF16 = jnp.bfloat16
LOG2E = math.log2(math.e)


def dot(a, b):
    return jnp.dot(a, b, preferred_element_type=F32)


def dot_nt(a, b):
    return lax.dot_general(a, b, NT, preferred_element_type=F32)


def halves(x):
    high = x.astype(BF16)
    return high, (x - high.astype(F32)).astype(BF16)


def dot3(a, b, product=dot):
    return product(a[0], b[0]) + (product(a[0], b[1]) + product(a[1], b[0]))


def lanes(shape):
    return lax.broadcasted_iota(jnp.int32, shape, len(shape) - 1)


def tiler(dim, width):
    row = lax.broadcasted_iota(jnp.int32, (dim, width), 0)
    return (row == lanes((dim, width)) % dim).astype(BF16)


def gather_kernel(
    heads,
    label_ref,
    tally_ref,
    x_ref,
    gain_ref,
    embed_ref,
    inputs_ref,
    score_ref,
    sharp_ref,
    shares_ref,
    sums_ref,
    ends_ref,
    end_ref,
    running_ref,
    inputs_t_ref,
    score_t_ref,
):
    step = pl.program_id(0)
    chunk, height, width = x_ref.shape
    points = chunk * height
    dim, parts = score_ref.shape
    half = width // 2
    group = heads // 2
    slots = label_ref.shape[0]

    @pl.when(step == 0)
    def _():
        running_ref[...] = jnp.zeros_like(running_ref)
        ends_ref[...] = jnp.zeros_like(ends_ref)
        inputs_t_ref[...] = inputs_ref[...].T
        tiled = lax.dot_general(
            score_ref[...],
            tiler(dim, width),
            (((0,), (0,)), ((), ())),
            preferred_element_type=F32,
        )
        lane = lanes((parts, width)) // dim
        for h in range(heads):
            score_t_ref[h * parts : (h + 1) * parts] = jnp.where(
                lane == h, tiled, 0.0
            ).astype(BF16)

        def note(i, carry):
            follower, last, order = carry
            k = slots - 1 - i
            here = label_ref[k]
            differs = here != label_ref[jnp.minimum(k + 1, slots - 1)]
            follower = jnp.where(differs, k, follower)
            order = order + differs.astype(jnp.int32)
            end_ref[k] = follower
            end_ref[slots + k] = order % chunk
            return follower, jnp.maximum(last, jnp.where(here < MESHES, here, -1)), order

        end_ref[2 * slots] = lax.fori_loop(
            0, slots, note, (jnp.int32(slots - 1), jnp.int32(-1), jnp.int32(0))
        )[1]

    x = x_ref[...].reshape(points, width).astype(F32)
    centre = x - jnp.mean(x, axis=1, keepdims=True)
    var = jnp.mean(centre * centre, axis=1, keepdims=True)
    normed = (centre * lax.rsqrt(var + 1e-05) * gain_ref[...]).astype(BF16)
    features = dot(normed, embed_ref[...]).astype(BF16)
    middles = dot_nt(inputs_t_ref[...], normed).astype(BF16)
    lane = lanes((1, height))
    living = jnp.concatenate(
        [
            (lane < tally_ref[step * chunk + b]).astype(F32)
            for b in range(chunk)
        ],
        axis=1,
    )
    for h in range(heads):
        rows = dot(
            score_t_ref[h * parts : (h + 1) * parts, h // group * half : (h // group + 1) * half],
            middles[h // group * half : (h // group + 1) * half],
        )
        top = jnp.max(rows, axis=0, keepdims=True)
        sharp = LOG2E / jnp.full((1, points), sharp_ref[h], F32)
        powers = jnp.exp2((rows - top) * sharp)
        scale = living / jnp.sum(powers, axis=0, keepdims=True)
        shares_ref[step, h * parts : (h + 1) * parts, :] = (powers * scale).astype(BF16)

    ones = jnp.ones((height, 128), BF16)
    share_lane = lanes((parts, half)) // dim
    total_lane = lanes((parts, 128))
    running = running_ref[...]
    for b in range(chunk):
        slot = step * chunk + b
        same = label_ref[slot] == label_ref[jnp.maximum(slot - 1, 0)]
        pieces = []
        totals = None
        for g in range(2):
            right = jnp.concatenate(
                [
                    features[b * height : (b + 1) * height, g * half : (g + 1) * half],
                    ones,
                ],
                axis=1,
            )
            got = dot(
                shares_ref[
                    step,
                    g * group * parts : (g + 1) * group * parts,
                    b * height : (b + 1) * height,
                ],
                right,
            )
            piece = got[:parts, :half]
            for i in range(group):
                mine = got[i * parts : (i + 1) * parts]
                piece = jnp.where(share_lane == i, mine[:, :half], piece)
                if totals is None:
                    totals = mine[:, half:]
                else:
                    totals = jnp.where(
                        total_lane == g * group + i, mine[:, half:], totals
                    )
            pieces.append(piece)
        running = jnp.where(same, running, 0.0) + jnp.concatenate(
            pieces + [totals], axis=1
        )
        sums_ref[b] = running
    running_ref[...] = running
    for b in range(chunk):
        slot = step * chunk + b
        label = label_ref[slot]
        stop = jnp.logical_and(label < MESHES, end_ref[slot] == slot)

        @pl.when(jnp.logical_and(stop, label == label_ref[0]))
        def _():
            ends_ref[0] = sums_ref[b]

        @pl.when(jnp.logical_and(stop, label == end_ref[2 * slots]))
        def _():
            ends_ref[1] = sums_ref[b]


def exchange_kernel(
    axes, heads, label_ref, end_ref, ends_ref, out_ref, held, sent, send_sem, recv_sem
):
    parts = out_ref.shape[1]
    width = out_ref.shape[2] - 128
    partners = []
    for name, size in reversed(axes):
        bit = 1
        while bit < size:
            at = {n: lax.axis_index(n) for n, _ in axes}
            here = at[name]
            at[name] = here + bit - 2 * bit * (here // bit % 2)
            partners.append(tuple(at[n] for n, _ in axes))
            bit *= 2
    barrier = pltpu.get_barrier_semaphore()
    for partner in partners:
        pl.semaphore_signal(barrier, inc=1, device_id=partner, device_id_type=MESH_ID)

    def own(i):
        totals = ends_ref[i, :, width:].T[:heads]
        totals = jnp.concatenate([totals, jnp.zeros((heads, width - parts), F32)], axis=1)
        full = jnp.concatenate([ends_ref[i, :, :width], totals], axis=0)
        return full.reshape(-1, 8, width)

    def put(i, k, values, ids):
        sent[i, k] = jnp.concatenate([values.reshape(-1, width), ids], axis=0).astype(BF16)

    def load(i, k):
        block = held[i, k].astype(F32)
        return block[: parts + heads].reshape(-1, 8, width), block[parts + heads :]

    first = group_first = own(0)
    last = group_last = own(1)
    ids = (8, width)
    first_id = group_first_id = jnp.full(ids, label_ref[0].astype(F32), F32)
    last_id = group_last_id = jnp.full(
        ids, end_ref[end_ref.shape[0] - 1].astype(F32), F32
    )
    put(0, 0, first, first_id)
    put(0, 1, last, last_id)
    pl.semaphore_wait(barrier, len(partners))
    for i, partner in enumerate(partners):
        copy = pltpu.make_async_remote_copy(
            src_ref=sent.at[i],
            dst_ref=held.at[i],
            send_sem=send_sem.at[i],
            recv_sem=recv_sem.at[i],
            device_id=partner,
            device_id_type=MESH_ID,
        )
        copy.start()
        copy.wait()
        other_first, other_first_id = load(i, 0)
        other_last, other_last_id = load(i, 1)
        if i < len(partners) - 1:
            new_first_id = jnp.minimum(group_first_id, other_first_id)
            new_last_id = jnp.maximum(group_last_id, other_last_id)
            group_first = jnp.where(
                (group_first_id == new_first_id)[None], group_first, 0.0
            ) + jnp.where((other_first_id == new_first_id)[None], other_first, 0.0)
            group_last = jnp.where(
                (group_last_id == new_last_id)[None], group_last, 0.0
            ) + jnp.where((other_last_id == new_last_id)[None], other_last, 0.0)
            group_first_id, group_last_id = new_first_id, new_last_id
            put(i + 1, 0, group_first, group_first_id)
            put(i + 1, 1, group_last, group_last_id)

    def found(i, own_id):
        other_first, other_first_id = load(i, 0)
        other_last, other_last_id = load(i, 1)
        return jnp.where(
            (own_id == other_first_id)[None],
            other_first,
            jnp.where((own_id == other_last_id)[None], other_last, 0.0),
        )

    for k, (total, own_id) in enumerate([(first, first_id), (last, last_id)]):
        for i in range(len(partners)):
            total = total + found(i, own_id)
        total = total.reshape(-1, width)
        rows = jnp.concatenate(
            [total[parts:, :128], jnp.zeros((128 - heads, 128), F32)], axis=0
        )
        out_ref[k] = jnp.concatenate([total[:parts], rows.T[:parts]], axis=1)


def spread_kernel(
    heads,
    label_ref,
    tally_ref,
    end_ref,
    x_ref,
    shares_ref,
    *refs,
):
    chunk, height, width = x_ref.shape
    sums_refs = refs[:chunk]
    ends_ref, maps_ref, readout_ref, out_ref, mixed_ref, map_ref = refs[chunk:]
    step = pl.program_id(0)
    parts = ends_ref.shape[1]
    dim = width // heads
    slots = label_ref.shape[0]
    last_label = end_ref[end_ref.shape[0] - 1]

    @pl.when(step == 0)
    def _():
        across = tiler(dim, width)
        row = lax.broadcasted_iota(jnp.int32, (width, dim), 0)
        down = (row % dim == lanes((width, dim))).astype(BF16)
        same = (
            lax.broadcasted_iota(jnp.int32, (width, width), 0) // dim
            == lanes((width, width)) // dim
        )
        for i in range(3):
            for j, part in enumerate(halves(maps_ref[i])):
                tall = dot(down, part) if i < 2 else dot_nt(down, part)
                map_ref[i, j] = jnp.where(same, dot(tall.astype(BF16), across), 0.0).astype(BF16)

    for b in range(chunk):
        slot = step * chunk + b
        label = label_ref[slot]
        fresh = jnp.logical_or(slot == 0, label != label_ref[jnp.maximum(slot - 1, 0)])

        @pl.when(jnp.logical_and(fresh, label < MESHES))
        def _():
            is_first = label == label_ref[0]
            is_last = label == last_label
            state = jnp.where(
                is_first,
                ends_ref[0],
                jnp.where(is_last, ends_ref[1], sums_refs[b][0]),
            )
            high, low = halves(state[:, width:])
            expand = (
                lax.broadcasted_iota(jnp.int32, (128, width), 0)
                == lanes((128, width)) // dim
            ).astype(BF16)
            totals = dot(high, expand) + dot(low, expand)
            tokens = state[:, :width] / (totals + 1.0)
            tokens = jnp.concatenate([tokens, tokens], axis=0)
            split = halves(tokens)
            maps = [(map_ref[i, 0], map_ref[i, 1]) for i in range(3)]
            queries = halves(dot3(split, maps[0]))
            keys = halves(dot3((split[0][:parts], split[1][:parts]), maps[1]))
            values = dot3(maps[2], split, dot_nt).astype(BF16)
            lane = lanes((parts, width)) // dim

            def stacked(k):
                return jnp.concatenate(
                    [jnp.where(lane == h, k, jnp.zeros_like(k)) for h in range(heads)],
                    axis=0,
                )

            scores = dot3(tuple(stacked(k) for k in keys), queries, dot_nt)
            probs = []
            factor = dim**-0.5 * LOG2E
            for h in range(heads):
                rows = scores[h * parts : (h + 1) * parts]
                top = jnp.max(rows, axis=0, keepdims=True)
                powers = jnp.exp2((rows - top) * factor)
                probs.append(powers / jnp.sum(powers, axis=0, keepdims=True))
            probs = jnp.concatenate(probs, axis=0).astype(BF16)
            row_head = lax.broadcasted_iota(jnp.int32, (width, 2 * parts), 0) // dim
            col_head = lanes((width, 2 * parts)) // parts

            def spaced(v):
                return jnp.concatenate(
                    [
                        jnp.where(row_head == col_head + 2 * t, v, jnp.zeros_like(v))
                        for t in range(heads // 2)
                    ],
                    axis=1,
                )

            mixed = dot(spaced(values), probs)
            mixed_ref[end_ref[slots + slot]] = spaced(mixed.astype(BF16))

    pieces = []
    for b in range(chunk):
        pieces.append(
            dot(
                mixed_ref[end_ref[slots + step * chunk + b]],
                shares_ref[step, :, b * height : (b + 1) * height],
            ).astype(BF16)
        )
    for b in range(chunk):
        projected = dot(pieces[b].T, readout_ref[...])
        row = lax.broadcasted_iota(jnp.int32, (height, width), 0)
        result = jnp.where(
            row < tally_ref[step * chunk + b], x_ref[b].astype(F32) + projected, 0.0
        )
        out_ref[b] = result.astype(BF16)


def whole(array):
    rank = array.ndim
    return pl.BlockSpec(array.shape, lambda *_: (0,) * rank)


def on_device(
    axes,
    vertex_values,
    label,
    tally,
    gain,
    embedding_matrix,
    partition_input_matrix,
    partition_score_matrix,
    sharpness,
    maps,
    readout_matrix,
):
    slots, height, width = vertex_values.shape
    heads = sharpness.shape[0]
    dim = width // heads
    parts = partition_score_matrix.shape[1]
    steps = slots // CHUNK
    wide = width + 128
    points = CHUNK * height
    gain = gain.reshape(1, width)
    x_spec = pl.BlockSpec((CHUNK, height, width), lambda i, *_: (i, 0, 0))
    shares_spec = pl.BlockSpec(memory_space=pltpu.VMEM)
    shares, sums, ends, end = pl.pallas_call(
        functools.partial(gather_kernel, heads),
        grid_spec=pltpu.PrefetchScalarGridSpec(
            num_scalar_prefetch=2,
            grid=(steps,),
            in_specs=[
                x_spec,
                whole(gain),
                whole(embedding_matrix),
                whole(partition_input_matrix),
                whole(partition_score_matrix),
                pl.BlockSpec(memory_space=pltpu.SMEM),
            ],
            out_specs=[
                shares_spec,
                pl.BlockSpec((CHUNK, parts, wide), lambda i, *_: (i, 0, 0)),
                pl.BlockSpec((2, parts, wide), lambda *_: (0, 0, 0)),
                pl.BlockSpec(memory_space=pltpu.SMEM),
            ],
            scratch_shapes=[
                pltpu.VMEM((parts, wide), F32),
                pltpu.VMEM((width, width), BF16),
                pltpu.VMEM((heads * parts, width), BF16),
            ],
        ),
        out_shape=[
            pltpu.VMEM((steps, heads * parts, points), BF16),
            jax.ShapeDtypeStruct((slots, parts, wide), F32),
            jax.ShapeDtypeStruct((2, parts, wide), F32),
            jax.ShapeDtypeStruct((2 * slots + 1,), jnp.int32),
        ],
        compiler_params=pltpu.CompilerParams(vmem_limit_bytes=47 << 20),
        name="gather",
    )(
        label,
        tally,
        vertex_values,
        gain,
        embedding_matrix,
        partition_input_matrix,
        partition_score_matrix,
        sharpness,
    )

    rounds = sum(size.bit_length() - 1 for _, size in axes)
    packet = (rounds, 2, parts + heads + 8, width)
    totals = pl.pallas_call(
        functools.partial(exchange_kernel, axes, heads),
        out_shape=jax.ShapeDtypeStruct((2, parts, wide), F32),
        in_specs=[
            pl.BlockSpec(memory_space=pltpu.SMEM),
            pl.BlockSpec(memory_space=pltpu.SMEM),
            pl.BlockSpec(memory_space=pltpu.VMEM),
        ],
        out_specs=pl.BlockSpec(memory_space=pltpu.VMEM),
        scratch_shapes=[
            pltpu.VMEM(packet, BF16),
            pltpu.VMEM(packet, BF16),
            pltpu.SemaphoreType.DMA((rounds,)),
            pltpu.SemaphoreType.DMA((rounds,)),
        ],
        compiler_params=pltpu.CompilerParams(
            collective_id=0, has_side_effects=True, vmem_limit_bytes=8 << 20
        ),
        name="exchange",
    )(label, end, ends)

    def sums_spec(b):
        return pl.BlockSpec(
            (1, parts, wide), lambda i, l, t, e: (e[i * CHUNK + b], 0, 0)
        )

    return pl.pallas_call(
        functools.partial(spread_kernel, heads),
        grid_spec=pltpu.PrefetchScalarGridSpec(
            num_scalar_prefetch=3,
            grid=(steps,),
            in_specs=[x_spec, shares_spec]
            + [sums_spec(b) for b in range(CHUNK)]
            + [
                whole(totals),
                whole(maps),
                whole(readout_matrix),
            ],
            out_specs=x_spec,
            scratch_shapes=[
                pltpu.VMEM((CHUNK, width, heads * parts), BF16),
                pltpu.VMEM((3, 2, width, width), BF16),
            ],
        ),
        out_shape=jax.ShapeDtypeStruct(vertex_values.shape, BF16),
        compiler_params=pltpu.CompilerParams(vmem_limit_bytes=47 << 20),
        name="spread",
    )(
        label,
        tally,
        end,
        vertex_values,
        shares,
        *([sums] * CHUNK),
        totals,
        maps,
        readout_matrix,
    )


def solution(mesh):
    axes = tuple((name, mesh.shape[name]) for name in mesh.axis_names)
    split = P(mesh.axis_names)
    points = P(mesh.axis_names, None, None)
    return jax.shard_map(
        functools.partial(on_device, axes),
        mesh=mesh,
        in_specs=(points, split, split) + (P(),) * 7,
        out_specs=points,
        check_vma=False,
    )
```

```python
import functools
import math

import jax
import jax.numpy as jnp
from jax import lax
from jax.experimental import pallas as pl
from jax.experimental.pallas import tpu as pltpu
from jax.sharding import PartitionSpec as P

MESHES = 64
CHUNK = 8
MESH_ID = pl.DeviceIdType.MESH
NT = (((1,), (1,)), ((), ()))
F32 = jnp.float32
BF16 = jnp.bfloat16
LOG2E = math.log2(math.e)


def dot(a, b):
    return jnp.dot(a, b, preferred_element_type=F32)


def dot_nt(a, b):
    return lax.dot_general(a, b, NT, preferred_element_type=F32)


def halves(x):
    high = x.astype(BF16)
    return high, (x - high.astype(F32)).astype(BF16)


def dot3(a, b, product=dot):
    return product(a[0], b[0]) + (product(a[0], b[1]) + product(a[1], b[0]))


def lanes(shape):
    return lax.broadcasted_iota(jnp.int32, shape, len(shape) - 1)


def tiler(dim, width):
    row = lax.broadcasted_iota(jnp.int32, (dim, width), 0)
    return (row == lanes((dim, width)) % dim).astype(BF16)


def gather_kernel(
    heads,
    label_ref,
    tally_ref,
    x_ref,
    gain_ref,
    embed_ref,
    inputs_ref,
    score_ref,
    sharp_ref,
    shares_ref,
    sums_ref,
    ends_ref,
    end_ref,
    running_ref,
    inputs_t_ref,
    score_t_ref,
):
    step = pl.program_id(0)
    chunk, height, width = x_ref.shape
    points = chunk * height
    dim, parts = score_ref.shape
    half = width // 2
    group = heads // 2
    slots = label_ref.shape[0]

    @pl.when(step == 0)
    def _():
        running_ref[...] = jnp.zeros_like(running_ref)
        ends_ref[...] = jnp.zeros_like(ends_ref)
        inputs_t_ref[...] = inputs_ref[...].T
        tiled = lax.dot_general(
            score_ref[...],
            tiler(dim, width),
            (((0,), (0,)), ((), ())),
            preferred_element_type=F32,
        )
        lane = lanes((parts, width)) // dim
        for h in range(heads):
            score_t_ref[h * parts : (h + 1) * parts] = jnp.where(
                lane == h, tiled, 0.0
            ).astype(BF16)

        def note(i, carry):
            follower, last, order = carry
            k = slots - 1 - i
            here = label_ref[k]
            differs = here != label_ref[jnp.minimum(k + 1, slots - 1)]
            follower = jnp.where(differs, k, follower)
            order = order + differs.astype(jnp.int32)
            end_ref[k] = follower
            end_ref[slots + k] = order % chunk
            return follower, jnp.maximum(last, jnp.where(here < MESHES, here, -1)), order

        end_ref[2 * slots] = lax.fori_loop(
            0, slots, note, (jnp.int32(slots - 1), jnp.int32(-1), jnp.int32(0))
        )[1]

    part_blocks = chunk // 2
    part_points = part_blocks * height
    lane = lanes((1, height))
    ones = jnp.ones((height, 128), BF16)
    share_lane = lanes((parts, half)) // dim
    total_lane = lanes((parts, 128))
    running = running_ref[...]
    features = []
    for s in range(2):
        x = x_ref[s * part_blocks : (s + 1) * part_blocks]
        x = x.reshape(part_points, width).astype(F32)
        centre = x - jnp.mean(x, axis=1, keepdims=True)
        var = jnp.mean(centre * centre, axis=1, keepdims=True)
        normed = (centre * lax.rsqrt(var + 1e-05) * gain_ref[...]).astype(BF16)
        features.append(dot(normed, embed_ref[...]).astype(BF16))
        middles = dot_nt(inputs_t_ref[...], normed).astype(BF16)
        living = jnp.concatenate(
            [
                (lane < tally_ref[step * chunk + s * part_blocks + b]).astype(F32)
                for b in range(part_blocks)
            ],
            axis=1,
        )
        for h in range(heads):
            rows = dot(
                score_t_ref[h * parts : (h + 1) * parts, h // group * half : (h // group + 1) * half],
                middles[h // group * half : (h // group + 1) * half],
            )
            top = jnp.max(rows, axis=0, keepdims=True)
            sharp = LOG2E / jnp.full((1, part_points), sharp_ref[h], F32)
            powers = jnp.exp2((rows - top) * sharp)
            scale = living / jnp.sum(powers, axis=0, keepdims=True)
            shares_ref[
                0, h * parts : (h + 1) * parts, s * part_points : (s + 1) * part_points
            ] = (powers * scale).astype(BF16)

    for b in range(chunk):
        slot = step * chunk + b
        same = label_ref[slot] == label_ref[jnp.maximum(slot - 1, 0)]
        row = b % part_blocks * height
        mine = features[b // part_blocks]
        pieces = []
        totals = None
        for g in range(2):
            right = jnp.concatenate(
                [mine[row : row + height, g * half : (g + 1) * half], ones], axis=1
            )
            piece = None
            for i in range(group):
                h = g * group + i
                got = dot(
                    shares_ref[
                        0, h * parts : (h + 1) * parts, b * height : (b + 1) * height
                    ],
                    right,
                )
                if piece is None:
                    piece = got[:, :half]
                else:
                    piece = jnp.where(share_lane == i, got[:, :half], piece)
                if totals is None:
                    totals = got[:, half:]
                else:
                    totals = jnp.where(total_lane == h, got[:, half:], totals)
            pieces.append(piece)
        running = jnp.where(same, running, 0.0) + jnp.concatenate(
            pieces + [totals], axis=1
        )
        sums_ref[b] = running
    running_ref[...] = running
    for b in range(chunk):
        slot = step * chunk + b
        label = label_ref[slot]
        stop = jnp.logical_and(label < MESHES, end_ref[slot] == slot)

        @pl.when(jnp.logical_and(stop, label == label_ref[0]))
        def _():
            ends_ref[0] = sums_ref[b]

        @pl.when(jnp.logical_and(stop, label == end_ref[2 * slots]))
        def _():
            ends_ref[1] = sums_ref[b]


def exchange_kernel(
    axes, heads, label_ref, end_ref, ends_ref, out_ref, held, sent, send_sem, recv_sem
):
    parts = out_ref.shape[1]
    width = out_ref.shape[2] - 128
    partners = []
    uppers = []
    for name, size in reversed(axes):
        bit = 1
        while bit < size:
            at = {n: lax.axis_index(n) for n, _ in axes}
            here = at[name]
            upper = here // bit % 2
            uppers.append(upper)
            at[name] = here + bit - 2 * bit * upper
            partners.append(tuple(at[n] for n, _ in axes))
            bit *= 2
    barrier = pltpu.get_barrier_semaphore()
    for partner in partners:
        pl.semaphore_signal(barrier, inc=1, device_id=partner, device_id_type=MESH_ID)

    def own(i):
        totals = ends_ref[i, :, width:].T[:heads]
        totals = jnp.concatenate([totals, jnp.zeros((heads, width - parts), F32)], axis=1)
        full = jnp.concatenate([ends_ref[i, :, :width], totals], axis=0)
        return full.reshape(-1, 8, width)

    def put(i, k, values, ids):
        sent[i, k] = jnp.concatenate([values.reshape(-1, width), ids], axis=0).astype(BF16)

    def load(i, k):
        block = held[i, k].astype(F32)
        return block[: parts + heads].reshape(-1, 8, width), block[parts + heads :]

    first = group_first = own(0)
    last = group_last = own(1)
    ids = (8, width)
    first_id = group_first_id = jnp.full(ids, label_ref[0].astype(F32), F32)
    last_id = group_last_id = jnp.full(
        ids, end_ref[end_ref.shape[0] - 1].astype(F32), F32
    )
    put(0, 0, first, first_id)
    put(0, 1, last, last_id)
    pl.semaphore_wait(barrier, len(partners))
    for i, partner in enumerate(partners):
        final = 0 < i == len(partners) - 1
        copy = pltpu.make_async_remote_copy(
            src_ref=sent.at[i, 0] if final else sent.at[i],
            dst_ref=held.at[i, 0] if final else held.at[i],
            send_sem=send_sem.at[i],
            recv_sem=recv_sem.at[i],
            device_id=partner,
            device_id_type=MESH_ID,
        )
        copy.start()
        copy.wait()
        if i < len(partners) - 1:
            other_first, other_first_id = load(i, 0)
            other_last, other_last_id = load(i, 1)
            new_first_id = jnp.minimum(group_first_id, other_first_id)
            new_last_id = jnp.maximum(group_last_id, other_last_id)
            group_first = jnp.where(
                (group_first_id == new_first_id)[None], group_first, 0.0
            ) + jnp.where((other_first_id == new_first_id)[None], other_first, 0.0)
            group_last = jnp.where(
                (group_last_id == new_last_id)[None], group_last, 0.0
            ) + jnp.where((other_last_id == new_last_id)[None], other_last, 0.0)
            group_first_id, group_last_id = new_first_id, new_last_id
            if i + 2 < len(partners):
                put(i + 1, 0, group_first, group_first_id)
                put(i + 1, 1, group_last, group_last_id)
            else:
                upper = uppers[i + 1] == 1
                put(
                    i + 1,
                    0,
                    jnp.where(upper, group_first, group_last),
                    jnp.where(upper, group_first_id, group_last_id),
                )

    def found(i, own_id):
        other_first, other_first_id = load(i, 0)
        if 0 < i == len(partners) - 1:
            return jnp.where((own_id == other_first_id)[None], other_first, 0.0)
        other_last, other_last_id = load(i, 1)
        return jnp.where(
            (own_id == other_first_id)[None],
            other_first,
            jnp.where((own_id == other_last_id)[None], other_last, 0.0),
        )

    for k, (total, own_id) in enumerate([(first, first_id), (last, last_id)]):
        for i in range(len(partners)):
            total = total + found(i, own_id)
        total = total.reshape(-1, width)
        rows = jnp.concatenate(
            [total[parts:, :128], jnp.zeros((128 - heads, 128), F32)], axis=0
        )
        out_ref[k] = jnp.concatenate([total[:parts], rows.T[:parts]], axis=1)


def spread_kernel(
    heads,
    label_ref,
    tally_ref,
    end_ref,
    x_ref,
    shares_ref,
    *refs,
):
    chunk, height, width = x_ref.shape
    sums_refs = refs[:chunk]
    ends_ref, maps_ref, readout_ref, out_ref, mixed_ref, map_ref = refs[chunk:]
    step = pl.program_id(0)
    parts = ends_ref.shape[1]
    dim = width // heads
    slots = label_ref.shape[0]
    last_label = end_ref[end_ref.shape[0] - 1]

    @pl.when(step == 0)
    def _():
        across = tiler(dim, width)
        row = lax.broadcasted_iota(jnp.int32, (width, dim), 0)
        down = (row % dim == lanes((width, dim))).astype(BF16)
        same = (
            lax.broadcasted_iota(jnp.int32, (width, width), 0) // dim
            == lanes((width, width)) // dim
        )
        for i in range(3):
            for j, part in enumerate(halves(maps_ref[i])):
                tall = dot(down, part) if i < 2 else dot_nt(down, part)
                map_ref[i, j] = jnp.where(same, dot(tall.astype(BF16), across), 0.0).astype(BF16)

    for b in range(chunk):
        slot = step * chunk + b
        label = label_ref[slot]
        fresh = jnp.logical_or(slot == 0, label != label_ref[jnp.maximum(slot - 1, 0)])

        @pl.when(jnp.logical_and(fresh, label < MESHES))
        def _():
            is_first = label == label_ref[0]
            is_last = label == last_label
            state = jnp.where(
                is_first,
                ends_ref[0],
                jnp.where(is_last, ends_ref[1], sums_refs[b][0]),
            )
            high, low = halves(state[:, width:])
            expand = (
                lax.broadcasted_iota(jnp.int32, (128, width), 0)
                == lanes((128, width)) // dim
            ).astype(BF16)
            totals = dot(high, expand) + dot(low, expand)
            tokens = state[:, :width] / (totals + 1.0)
            tokens = jnp.concatenate([tokens, tokens], axis=0)
            split = halves(tokens)
            maps = [(map_ref[i, 0], map_ref[i, 1]) for i in range(3)]
            queries = halves(dot3(split, maps[0]))
            keys = halves(dot3((split[0][:parts], split[1][:parts]), maps[1]))
            values = dot3(maps[2], split, dot_nt).astype(BF16)
            lane = lanes((parts, width)) // dim

            def stacked(k):
                return jnp.concatenate(
                    [jnp.where(lane == h, k, jnp.zeros_like(k)) for h in range(heads)],
                    axis=0,
                )

            scores = dot3(tuple(stacked(k) for k in keys), queries, dot_nt)
            probs = []
            factor = dim**-0.5 * LOG2E
            for h in range(heads):
                rows = scores[h * parts : (h + 1) * parts]
                top = jnp.max(rows, axis=0, keepdims=True)
                powers = jnp.exp2((rows - top) * factor)
                probs.append(powers / jnp.sum(powers, axis=0, keepdims=True))
            probs = jnp.concatenate(probs, axis=0).astype(BF16)
            row_head = lax.broadcasted_iota(jnp.int32, (width, 2 * parts), 0) // dim
            col_head = lanes((width, 2 * parts)) // parts

            def spaced(v):
                return jnp.concatenate(
                    [
                        jnp.where(row_head == col_head + 2 * t, v, jnp.zeros_like(v))
                        for t in range(heads // 2)
                    ],
                    axis=1,
                )

            mixed = dot(spaced(values), probs)
            mixed_ref[end_ref[slots + slot]] = spaced(mixed.astype(BF16))

    pieces = []
    for b in range(chunk):
        pieces.append(
            dot(
                mixed_ref[end_ref[slots + step * chunk + b]],
                shares_ref[0, :, b * height : (b + 1) * height],
            ).astype(BF16)
        )
    for b in range(chunk):
        projected = dot(pieces[b].T, readout_ref[...])
        row = lax.broadcasted_iota(jnp.int32, (height, width), 0)
        result = jnp.where(
            row < tally_ref[step * chunk + b], x_ref[b].astype(F32) + projected, 0.0
        )
        out_ref[b] = result.astype(BF16)


def whole(array):
    rank = array.ndim
    return pl.BlockSpec(array.shape, lambda *_: (0,) * rank)


def on_device(
    axes,
    vertex_values,
    label,
    tally,
    gain,
    embedding_matrix,
    partition_input_matrix,
    partition_score_matrix,
    sharpness,
    maps,
    readout_matrix,
):
    slots, height, width = vertex_values.shape
    heads = sharpness.shape[0]
    dim = width // heads
    parts = partition_score_matrix.shape[1]
    steps = slots // CHUNK
    wide = width + 128
    points = CHUNK * height
    gain = gain.reshape(1, width)
    x_spec = pl.BlockSpec((CHUNK, height, width), lambda i, *_: (i, 0, 0))
    shares_spec = pl.BlockSpec((1, heads * parts, points), lambda i, *_: (i, 0, 0))
    shares, sums, ends, end = pl.pallas_call(
        functools.partial(gather_kernel, heads),
        grid_spec=pltpu.PrefetchScalarGridSpec(
            num_scalar_prefetch=2,
            grid=(steps,),
            in_specs=[
                x_spec,
                whole(gain),
                whole(embedding_matrix),
                whole(partition_input_matrix),
                whole(partition_score_matrix),
                pl.BlockSpec(memory_space=pltpu.SMEM),
            ],
            out_specs=[
                shares_spec,
                pl.BlockSpec((CHUNK, parts, wide), lambda i, *_: (i, 0, 0)),
                pl.BlockSpec((2, parts, wide), lambda *_: (0, 0, 0)),
                pl.BlockSpec(memory_space=pltpu.SMEM),
            ],
            scratch_shapes=[
                pltpu.VMEM((parts, wide), F32),
                pltpu.VMEM((width, width), BF16),
                pltpu.VMEM((heads * parts, width), BF16),
            ],
        ),
        out_shape=[
            jax.ShapeDtypeStruct((steps, heads * parts, points), BF16),
            jax.ShapeDtypeStruct((slots, parts, wide), F32),
            jax.ShapeDtypeStruct((2, parts, wide), F32),
            jax.ShapeDtypeStruct((2 * slots + 1,), jnp.int32),
        ],
        name="gather",
    )(
        label,
        tally,
        vertex_values,
        gain,
        embedding_matrix,
        partition_input_matrix,
        partition_score_matrix,
        sharpness,
    )

    rounds = sum(size.bit_length() - 1 for _, size in axes)
    packet = (rounds, 2, parts + heads + 8, width)
    totals = pl.pallas_call(
        functools.partial(exchange_kernel, axes, heads),
        out_shape=jax.ShapeDtypeStruct((2, parts, wide), F32),
        in_specs=[
            pl.BlockSpec(memory_space=pltpu.SMEM),
            pl.BlockSpec(memory_space=pltpu.SMEM),
            pl.BlockSpec(memory_space=pltpu.VMEM),
        ],
        out_specs=pl.BlockSpec(memory_space=pltpu.VMEM),
        scratch_shapes=[
            pltpu.VMEM(packet, BF16),
            pltpu.VMEM(packet, BF16),
            pltpu.SemaphoreType.DMA((rounds,)),
            pltpu.SemaphoreType.DMA((rounds,)),
        ],
        compiler_params=pltpu.CompilerParams(collective_id=0, has_side_effects=True),
        name="exchange",
    )(label, end, ends)

    def sums_spec(b):
        return pl.BlockSpec(
            (1, parts, wide), lambda i, l, t, e: (e[i * CHUNK + b], 0, 0)
        )

    return pl.pallas_call(
        functools.partial(spread_kernel, heads),
        grid_spec=pltpu.PrefetchScalarGridSpec(
            num_scalar_prefetch=3,
            grid=(steps,),
            in_specs=[x_spec, shares_spec]
            + [sums_spec(b) for b in range(CHUNK)]
            + [
                whole(totals),
                whole(maps),
                whole(readout_matrix),
            ],
            out_specs=x_spec,
            scratch_shapes=[
                pltpu.VMEM((CHUNK, width, heads * parts), BF16),
                pltpu.VMEM((3, 2, width, width), BF16),
            ],
        ),
        out_shape=jax.ShapeDtypeStruct(vertex_values.shape, BF16),
        name="spread",
    )(
        label,
        tally,
        end,
        vertex_values,
        shares,
        *([sums] * CHUNK),
        totals,
        maps,
        readout_matrix,
    )


def solution(mesh):
    axes = tuple((name, mesh.shape[name]) for name in mesh.axis_names)
    split = P(mesh.axis_names)
    points = P(mesh.axis_names, None, None)
    return jax.shard_map(
        functools.partial(on_device, axes),
        mesh=mesh,
        in_specs=(points, split, split) + (P(),) * 7,
        out_specs=points,
        check_vma=False,
    )
```

```python
import functools
import math

import jax
import jax.numpy as jnp
from jax import lax
from jax.experimental import pallas as pl
from jax.experimental.pallas import tpu as pltpu
from jax.sharding import PartitionSpec as P

MESHES = 64
CHUNK = 8
MESH_ID = pl.DeviceIdType.MESH
NT = (((1,), (1,)), ((), ()))
F32 = jnp.float32
BF16 = jnp.bfloat16
LOG2E = math.log2(math.e)


def dot(a, b):
    return jnp.dot(a, b, preferred_element_type=F32)


def dot_nt(a, b):
    return lax.dot_general(a, b, NT, preferred_element_type=F32)


def halves(x):
    high = x.astype(BF16)
    return high, (x - high.astype(F32)).astype(BF16)


def dot3(a, b, product=dot):
    return product(a[0], b[0]) + (product(a[0], b[1]) + product(a[1], b[0]))


def lanes(shape):
    return lax.broadcasted_iota(jnp.int32, shape, len(shape) - 1)


def tiler(dim, width):
    row = lax.broadcasted_iota(jnp.int32, (dim, width), 0)
    return (row == lanes((dim, width)) % dim).astype(BF16)


def gather_kernel(
    heads,
    label_ref,
    tally_ref,
    x_ref,
    gain_ref,
    embed_ref,
    inputs_ref,
    score_ref,
    sharp_ref,
    shares_ref,
    sums_ref,
    ends_ref,
    end_ref,
    running_ref,
    inputs_t_ref,
    score_t_ref,
):
    step = pl.program_id(0)
    chunk, height, width = x_ref.shape
    points = chunk * height
    dim, parts = score_ref.shape
    half = width // 2
    group = heads // 2
    slots = label_ref.shape[0]

    @pl.when(step == 0)
    def _():
        running_ref[...] = jnp.zeros_like(running_ref)
        ends_ref[...] = jnp.zeros_like(ends_ref)
        inputs_t_ref[...] = inputs_ref[...].T
        tiled = lax.dot_general(
            score_ref[...],
            tiler(dim, width),
            (((0,), (0,)), ((), ())),
            preferred_element_type=F32,
        )
        lane = lanes((parts, width)) // dim
        for h in range(heads):
            score_t_ref[h * parts : (h + 1) * parts] = jnp.where(
                lane == h, tiled, 0.0
            ).astype(BF16)

        def note(i, carry):
            follower, last, order = carry
            k = slots - 1 - i
            here = label_ref[k]
            differs = here != label_ref[jnp.minimum(k + 1, slots - 1)]
            follower = jnp.where(differs, k, follower)
            order = order + differs.astype(jnp.int32)
            end_ref[k] = follower
            end_ref[slots + k] = order % chunk
            return follower, jnp.maximum(last, jnp.where(here < MESHES, here, -1)), order

        end_ref[2 * slots] = lax.fori_loop(
            0, slots, note, (jnp.int32(slots - 1), jnp.int32(-1), jnp.int32(0))
        )[1]

    part_blocks = chunk // 2
    part_points = part_blocks * height
    lane = lanes((1, height))
    ones = jnp.ones((height, 128), BF16)
    share_lane = lanes((parts, half)) // dim
    total_lane = lanes((parts, 128))
    running = running_ref[...]
    features = []
    for s in range(2):
        x = x_ref[s * part_blocks : (s + 1) * part_blocks]
        x = x.reshape(part_points, width).astype(F32)
        centre = x - jnp.mean(x, axis=1, keepdims=True)
        var = jnp.mean(centre * centre, axis=1, keepdims=True)
        normed = (centre * lax.rsqrt(var + 1e-05) * gain_ref[...]).astype(BF16)
        features.append(dot(normed, embed_ref[...]).astype(BF16))
        middles = dot_nt(inputs_t_ref[...], normed).astype(BF16)
        living = jnp.concatenate(
            [
                (lane < tally_ref[step * chunk + s * part_blocks + b]).astype(F32)
                for b in range(part_blocks)
            ],
            axis=1,
        )
        for h in range(heads):
            rows = dot(
                score_t_ref[h * parts : (h + 1) * parts, h // group * half : (h // group + 1) * half],
                middles[h // group * half : (h // group + 1) * half],
            )
            top = jnp.max(rows, axis=0, keepdims=True)
            sharp = LOG2E / jnp.full((1, part_points), sharp_ref[h], F32)
            powers = jnp.exp2((rows - top) * sharp)
            scale = living / jnp.sum(powers, axis=0, keepdims=True)
            shares_ref[
                0, h * parts : (h + 1) * parts, s * part_points : (s + 1) * part_points
            ] = (powers * scale).astype(BF16)

    for b in range(chunk):
        slot = step * chunk + b
        same = label_ref[slot] == label_ref[jnp.maximum(slot - 1, 0)]
        row = b % part_blocks * height
        mine = features[b // part_blocks]
        pieces = []
        totals = None
        for g in range(2):
            right = jnp.concatenate(
                [mine[row : row + height, g * half : (g + 1) * half], ones], axis=1
            )
            piece = None
            for i in range(group):
                h = g * group + i
                got = dot(
                    shares_ref[
                        0, h * parts : (h + 1) * parts, b * height : (b + 1) * height
                    ],
                    right,
                )
                if piece is None:
                    piece = got[:, :half]
                else:
                    piece = jnp.where(share_lane == i, got[:, :half], piece)
                if totals is None:
                    totals = got[:, half:]
                else:
                    totals = jnp.where(total_lane == h, got[:, half:], totals)
            pieces.append(piece)
        running = jnp.where(same, running, 0.0) + jnp.concatenate(
            pieces + [totals], axis=1
        )
        sums_ref[b] = running
    running_ref[...] = running
    for b in range(chunk):
        slot = step * chunk + b
        label = label_ref[slot]
        stop = jnp.logical_and(label < MESHES, end_ref[slot] == slot)

        @pl.when(jnp.logical_and(stop, label == label_ref[0]))
        def _():
            ends_ref[0] = sums_ref[b]

        @pl.when(jnp.logical_and(stop, label == end_ref[2 * slots]))
        def _():
            ends_ref[1] = sums_ref[b]


def exchange_kernel(
    axes, heads, label_ref, end_ref, ends_ref, out_ref, held, sent, send_sem, recv_sem
):
    parts = out_ref.shape[1]
    width = out_ref.shape[2] - 128
    partners = []
    uppers = []
    for name, size in reversed(axes):
        bit = 1
        while bit < size:
            at = {n: lax.axis_index(n) for n, _ in axes}
            here = at[name]
            upper = here // bit % 2
            uppers.append(upper)
            at[name] = here + bit - 2 * bit * upper
            partners.append(tuple(at[n] for n, _ in axes))
            bit *= 2
    barrier = pltpu.get_barrier_semaphore()
    for partner in partners:
        pl.semaphore_signal(barrier, inc=1, device_id=partner, device_id_type=MESH_ID)

    def own(i):
        totals = ends_ref[i, :, width:].T[:heads]
        totals = jnp.concatenate([totals, jnp.zeros((heads, width - parts), F32)], axis=1)
        full = jnp.concatenate([ends_ref[i, :, :width], totals], axis=0)
        return full.reshape(-1, 8, width)

    def put(i, k, values, ids):
        sent[i, k] = jnp.concatenate([values.reshape(-1, width), ids], axis=0).astype(BF16)

    def load(i, k):
        block = held[i, k].astype(F32)
        return block[: parts + heads].reshape(-1, 8, width), block[parts + heads :]

    first = group_first = own(0)
    last = group_last = own(1)
    ids = (8, width)
    first_id = group_first_id = jnp.full(ids, label_ref[0].astype(F32), F32)
    last_id = group_last_id = jnp.full(
        ids, end_ref[end_ref.shape[0] - 1].astype(F32), F32
    )
    put(0, 0, first, first_id)
    put(0, 1, last, last_id)
    pl.semaphore_wait(barrier, len(partners))
    for i, partner in enumerate(partners):
        final = 0 < i == len(partners) - 1
        copy = pltpu.make_async_remote_copy(
            src_ref=sent.at[i, 0] if final else sent.at[i],
            dst_ref=held.at[i, 0] if final else held.at[i],
            send_sem=send_sem.at[i],
            recv_sem=recv_sem.at[i],
            device_id=partner,
            device_id_type=MESH_ID,
        )
        copy.start()
        copy.wait()
        if i < len(partners) - 1:
            other_first, other_first_id = load(i, 0)
            other_last, other_last_id = load(i, 1)
            new_first_id = jnp.minimum(group_first_id, other_first_id)
            new_last_id = jnp.maximum(group_last_id, other_last_id)
            group_first = jnp.where(
                (group_first_id == new_first_id)[None], group_first, 0.0
            ) + jnp.where((other_first_id == new_first_id)[None], other_first, 0.0)
            group_last = jnp.where(
                (group_last_id == new_last_id)[None], group_last, 0.0
            ) + jnp.where((other_last_id == new_last_id)[None], other_last, 0.0)
            group_first_id, group_last_id = new_first_id, new_last_id
            if i + 2 < len(partners):
                put(i + 1, 0, group_first, group_first_id)
                put(i + 1, 1, group_last, group_last_id)
            else:
                upper = uppers[i + 1] == 1
                put(
                    i + 1,
                    0,
                    jnp.where(upper, group_first, group_last),
                    jnp.where(upper, group_first_id, group_last_id),
                )

    def found(i, own_id):
        other_first, other_first_id = load(i, 0)
        if 0 < i == len(partners) - 1:
            return jnp.where((own_id == other_first_id)[None], other_first, 0.0)
        other_last, other_last_id = load(i, 1)
        return jnp.where(
            (own_id == other_first_id)[None],
            other_first,
            jnp.where((own_id == other_last_id)[None], other_last, 0.0),
        )

    for k, (total, own_id) in enumerate([(first, first_id), (last, last_id)]):
        for i in range(len(partners)):
            total = total + found(i, own_id)
        total = total.reshape(-1, width)
        rows = jnp.concatenate(
            [total[parts:, :128], jnp.zeros((128 - heads, 128), F32)], axis=0
        )
        out_ref[k] = jnp.concatenate([total[:parts], rows.T[:parts]], axis=1)


def spread_kernel(
    heads,
    label_ref,
    tally_ref,
    end_ref,
    x_ref,
    shares_ref,
    *refs,
):
    chunk, height, width = x_ref.shape
    sums_refs = refs[:chunk]
    ends_ref, maps_ref, readout_ref, out_ref, mixed_ref, map_ref = refs[chunk:]
    step = pl.program_id(0)
    parts = ends_ref.shape[1]
    dim = width // heads
    slots = label_ref.shape[0]
    last_label = end_ref[end_ref.shape[0] - 1]

    @pl.when(step == 0)
    def _():
        across = tiler(dim, width)
        row = lax.broadcasted_iota(jnp.int32, (width, dim), 0)
        down = (row % dim == lanes((width, dim))).astype(BF16)
        same = (
            lax.broadcasted_iota(jnp.int32, (width, width), 0) // dim
            == lanes((width, width)) // dim
        )
        for i in range(3):
            for j, part in enumerate(halves(maps_ref[i])):
                tall = dot(down, part) if i < 2 else dot_nt(down, part)
                map_ref[i, j] = jnp.where(same, dot(tall.astype(BF16), across), 0.0).astype(BF16)

    for b in range(chunk):
        slot = step * chunk + b
        label = label_ref[slot]
        fresh = jnp.logical_or(slot == 0, label != label_ref[jnp.maximum(slot - 1, 0)])

        @pl.when(jnp.logical_and(fresh, label < MESHES))
        def _():
            is_first = label == label_ref[0]
            is_last = label == last_label
            state = jnp.where(
                is_first,
                ends_ref[0],
                jnp.where(is_last, ends_ref[1], sums_refs[b][0]),
            )
            high, low = halves(state[:, width:])
            expand = (
                lax.broadcasted_iota(jnp.int32, (128, width), 0)
                == lanes((128, width)) // dim
            ).astype(BF16)
            totals = dot(high, expand) + dot(low, expand)
            tokens = state[:, :width] / (totals + 1.0)
            tokens = jnp.concatenate([tokens, tokens], axis=0)
            split = halves(tokens)
            maps = [(map_ref[i, 0], map_ref[i, 1]) for i in range(3)]
            queries = halves(dot3(split, maps[0]))
            keys = halves(dot3((split[0][:parts], split[1][:parts]), maps[1]))
            values = dot3(maps[2], split, dot_nt).astype(BF16)
            group = heads // 2
            half = width // 2
            lane = lanes((parts, width)) // dim % group
            scores = []
            for g in range(2):
                at = slice(g * half, (g + 1) * half)
                pair = jnp.concatenate([keys[0][:, at], keys[1][:, at]], axis=1)
                left = jnp.concatenate(
                    [jnp.where(lane == i, pair, jnp.zeros_like(pair)) for i in range(group)],
                    axis=0,
                )
                high, low = queries[0][:, at], queries[1][:, at]
                scores.append(
                    dot_nt(left, jnp.concatenate([high, high], axis=1))
                    + dot_nt(left[:, :half], low)
                )
            scores = jnp.concatenate(scores, axis=0)
            probs = []
            factor = dim**-0.5 * LOG2E
            for h in range(heads):
                rows = scores[h * parts : (h + 1) * parts]
                top = jnp.max(rows, axis=0, keepdims=True)
                powers = jnp.exp2((rows - top) * factor)
                probs.append(powers / jnp.sum(powers, axis=0, keepdims=True))
            probs = jnp.concatenate(probs, axis=0).astype(BF16)
            row_head = lax.broadcasted_iota(jnp.int32, (width, 2 * parts), 0) // dim
            col_head = lanes((width, 2 * parts)) // parts

            def spaced(v):
                return jnp.concatenate(
                    [
                        jnp.where(row_head == col_head + 2 * t, v, jnp.zeros_like(v))
                        for t in range(heads // 2)
                    ],
                    axis=1,
                )

            mixed = dot(spaced(values), probs)
            mixed_ref[end_ref[slots + slot]] = spaced(mixed.astype(BF16))

    pieces = []
    for b in range(chunk):
        pieces.append(
            dot(
                mixed_ref[end_ref[slots + step * chunk + b]],
                shares_ref[0, :, b * height : (b + 1) * height],
            ).astype(BF16)
        )
    for b in range(chunk):
        projected = dot(pieces[b].T, readout_ref[...])
        row = lax.broadcasted_iota(jnp.int32, (height, width), 0)
        result = jnp.where(
            row < tally_ref[step * chunk + b], x_ref[b].astype(F32) + projected, 0.0
        )
        out_ref[b] = result.astype(BF16)


def whole(array):
    rank = array.ndim
    return pl.BlockSpec(array.shape, lambda *_: (0,) * rank)


def on_device(
    axes,
    vertex_values,
    label,
    tally,
    gain,
    embedding_matrix,
    partition_input_matrix,
    partition_score_matrix,
    sharpness,
    maps,
    readout_matrix,
):
    slots, height, width = vertex_values.shape
    heads = sharpness.shape[0]
    dim = width // heads
    parts = partition_score_matrix.shape[1]
    steps = slots // CHUNK
    wide = width + 128
    points = CHUNK * height
    gain = gain.reshape(1, width)
    x_spec = pl.BlockSpec((CHUNK, height, width), lambda i, *_: (i, 0, 0))
    shares_spec = pl.BlockSpec((1, heads * parts, points), lambda i, *_: (i, 0, 0))
    shares, sums, ends, end = pl.pallas_call(
        functools.partial(gather_kernel, heads),
        grid_spec=pltpu.PrefetchScalarGridSpec(
            num_scalar_prefetch=2,
            grid=(steps,),
            in_specs=[
                x_spec,
                whole(gain),
                whole(embedding_matrix),
                whole(partition_input_matrix),
                whole(partition_score_matrix),
                pl.BlockSpec(memory_space=pltpu.SMEM),
            ],
            out_specs=[
                shares_spec,
                pl.BlockSpec((CHUNK, parts, wide), lambda i, *_: (i, 0, 0)),
                pl.BlockSpec((2, parts, wide), lambda *_: (0, 0, 0)),
                pl.BlockSpec(memory_space=pltpu.SMEM),
            ],
            scratch_shapes=[
                pltpu.VMEM((parts, wide), F32),
                pltpu.VMEM((width, width), BF16),
                pltpu.VMEM((heads * parts, width), BF16),
            ],
        ),
        out_shape=[
            jax.ShapeDtypeStruct((steps, heads * parts, points), BF16),
            jax.ShapeDtypeStruct((slots, parts, wide), F32),
            jax.ShapeDtypeStruct((2, parts, wide), F32),
            jax.ShapeDtypeStruct((2 * slots + 1,), jnp.int32),
        ],
        compiler_params=pltpu.CompilerParams(),
        name="gather",
    )(
        label,
        tally,
        vertex_values,
        gain,
        embedding_matrix,
        partition_input_matrix,
        partition_score_matrix,
        sharpness,
    )

    rounds = sum(size.bit_length() - 1 for _, size in axes)
    packet = (rounds, 2, parts + heads + 8, width)
    totals = pl.pallas_call(
        functools.partial(exchange_kernel, axes, heads),
        out_shape=jax.ShapeDtypeStruct((2, parts, wide), F32),
        in_specs=[
            pl.BlockSpec(memory_space=pltpu.SMEM),
            pl.BlockSpec(memory_space=pltpu.SMEM),
            pl.BlockSpec(memory_space=pltpu.VMEM),
        ],
        out_specs=pl.BlockSpec(memory_space=pltpu.VMEM),
        scratch_shapes=[
            pltpu.VMEM(packet, BF16),
            pltpu.VMEM(packet, BF16),
            pltpu.SemaphoreType.DMA((rounds,)),
            pltpu.SemaphoreType.DMA((rounds,)),
        ],
        compiler_params=pltpu.CompilerParams(collective_id=0, has_side_effects=True),
        name="exchange",
    )(label, end, ends)

    def sums_spec(b):
        return pl.BlockSpec(
            (1, parts, wide), lambda i, l, t, e: (e[i * CHUNK + b], 0, 0)
        )

    return pl.pallas_call(
        functools.partial(spread_kernel, heads),
        grid_spec=pltpu.PrefetchScalarGridSpec(
            num_scalar_prefetch=3,
            grid=(steps,),
            in_specs=[x_spec, shares_spec]
            + [sums_spec(b) for b in range(CHUNK)]
            + [
                whole(totals),
                whole(maps),
                whole(readout_matrix),
            ],
            out_specs=x_spec,
            scratch_shapes=[
                pltpu.VMEM((CHUNK, width, heads * parts), BF16),
                pltpu.VMEM((3, 2, width, width), BF16),
            ],
        ),
        out_shape=jax.ShapeDtypeStruct(vertex_values.shape, BF16),
        name="spread",
    )(
        label,
        tally,
        end,
        vertex_values,
        shares,
        *([sums] * CHUNK),
        totals,
        maps,
        readout_matrix,
    )


def solution(mesh):
    axes = tuple((name, mesh.shape[name]) for name in mesh.axis_names)
    split = P(mesh.axis_names)
    points = P(mesh.axis_names, None, None)
    return jax.shard_map(
        functools.partial(on_device, axes),
        mesh=mesh,
        in_specs=(points, split, split) + (P(),) * 7,
        out_specs=points,
        check_vma=False,
    )
```
